32 devices in a mesh: dp: 16 (over z, x, core), tensor: 2 (over y).
Axes of the slice: x: 2, y: 2, z: 4, core: 2. Of those that a mesh axis runs over, the one named last changes fastest.
Arguments:
- x_in: bfloat16 [16384, 2048], P('dp'), may hold values from -6 to 6
- norm_gain: float32 [2048], replicated, may hold values from 0.5 to 1.5
- w_zx: bfloat16 [2048, 2, 4096], P(None, None, 'tensor'), may hold values from -0.125 to 0.125
- w_bc: bfloat16 [2048, 256], replicated, may hold values from -0.125 to 0.125
- w_dt: bfloat16 [2048, 64], P(None, 'tensor'), may hold values from -0.125 to 0.125
- conv_x: float32 [5, 4096], P(None, 'tensor'), may hold values from -3 to 3
- conv_bc: float32 [5, 256], replicated, may hold values from -3 to 3
- dt_bias: float32 [64], P('tensor'), may hold values from -4 to -1
- a_log: float32 [64], P('tensor'), may hold values from -3 to 1.5
- d_skip: float32 [64], P('tensor'), may hold values from 0.5 to 1.5
- gate_gain: float32 [4096], P('tensor'), may hold values from 0.5 to 1.5
- w_out: bfloat16 [4096, 2048], P('tensor'), may hold values from -0.09375 to 0.09375
- cotangent: bfloat16 [16384, 2048], P('dp'), may hold values from -6 to 6
- block_parent: int32 [128], P('dp'), may hold values from -1 to 6, as said below
Outputs:
- mixed: bfloat16 [16384, 2048], P('dp')
- input_grad: bfloat16 [16384, 2048], P('dp')
- norm_gain_grad: float32 [2048], replicated
- w_zx_grad: float32 [2048, 2, 4096], P('dp', None, 'tensor')
- w_bc_grad: float32 [2048, 256], replicated
- w_dt_grad: float32 [2048, 64], P('dp', 'tensor')
- conv_x_grad: float32 [5, 4096], P(None, 'tensor')
- conv_bc_grad: float32 [5, 256], replicated
- dt_bias_grad: float32 [64], P('tensor')
- a_log_grad: float32 [64], P('tensor')
- d_skip_grad: float32 [64], P('tensor')
- gate_gain_grad: float32 [4096], P('tensor')
- w_out_grad: float32 [4096, 2048], P('tensor', 'dp')
The draws below stay inside these ranges and needn't reach their ends.
Inputs may be any that keep to these rules, and one draw needn't show every extreme that they name: `block_parent`: each device's 8 blocks hold one tree. A block's entry is the index, among its device's blocks, of an earlier block whose last token precedes its first token, or -1 at the root; the first half of the blocks or more form a chain from the root, and the last block continues the block before it.
All inputs are finite; a program needn't handle non-finite values.
Results may differ from the reference program's by a relative error of at most 0.014.
Values may be sent and summed in bfloat16 or wider, within the bound.
No kernel may reach another device: no remote copies, remote signals or barrier semaphores. Data moves between devices by JAX's collectives and lax.ppermute only.
A program may use at most 320 MiB of HBM per device.

```python
import jax
import jax.numpy as jnp
from jax import lax

D = 2048
HEADS = 64
STATE = 128
CONV = 4
BLOCKS = 8
DI = 4096
TOKENS = 16384
ALL_BLOCKS = 128
N_DP = 16


def draw_block_parent(key, part):
    devices = ALL_BLOCKS // BLOCKS
    trunk_key, branch_key = jax.random.split(key)
    trunk_len = jax.random.randint(trunk_key, (devices, 1), (BLOCKS + 1) // 2, BLOCKS)
    position = jnp.arange(BLOCKS, dtype=jnp.int32)[None, :]
    random_bits = jax.random.randint(branch_key, (devices, BLOCKS), 0, 1048576)
    branch_parent = random_bits % jnp.maximum(position, 1)
    parents = jnp.where(position < trunk_len, position - 1, branch_parent)
    parents = jnp.where(position == BLOCKS - 1, BLOCKS - 2, parents)
    return parents.reshape(-1).astype(jnp.int32)


def levels(key, extent, cuts, low, largest):
    gain = 1.0
    for axis_at, parts in cuts:
        heights = jax.random.uniform(jax.random.fold_in(jax.random.fold_in(key, 6), axis_at), (parts,), jnp.float32, low / len(cuts), largest / len(cuts))
        gain = gain * jnp.repeat(jnp.exp(heights), extent[axis_at] // parts).reshape((-1,) + (1,) * (len(extent) - 1 - axis_at))
    return gain


def centred(own_key, extent, deviation, limit, cuts=(), kind=jnp.bfloat16):
    array = deviation * jax.random.normal(own_key, extent, jnp.float32)
    if cuts:
        array = array * levels(own_key, extent, cuts, -0.22, 0.18)
    return jnp.clip(array, -limit, limit).astype(kind)


def setup_inputs(seed: int = 0) -> dict:
    splits = jax.random.split(jax.random.key(seed), 15)
    return {
        "x_in": centred(splits[0], (TOKENS, D), 1.0, 6.0, ((0, 16),)),
        "norm_gain": jnp.clip(1.0 + 0.1 * jax.random.normal(splits[1], (D,), jnp.float32), 0.5, 1.5),
        "w_zx": centred(splits[2], (D, 2, DI), D ** -0.5, 0.125, ((2, 2),)),
        "w_bc": centred(splits[3], (D, 2 * STATE), D ** -0.5, 0.125),
        "w_dt": centred(splits[4], (D, HEADS), D ** -0.5, 0.125, ((1, 2),)),
        "conv_x": centred(splits[5], (CONV + 1, DI), 0.5, 3.0, ((1, 2),), jnp.float32),
        "conv_bc": centred(splits[6], (CONV + 1, 2 * STATE), 0.5, 3.0, (), jnp.float32),
        "dt_bias": jnp.clip(-4.0 + 3.0 * jax.random.uniform(splits[7], (HEADS,), jnp.float32) ** levels(splits[7], (HEADS,), ((0, 2),), -0.2, 0.2), -4.0, -1.0),
        "a_log": jnp.clip(-3.0 + 4.5 * jax.random.uniform(splits[8], (HEADS,), jnp.float32) ** levels(splits[8], (HEADS,), ((0, 2),), -0.2, 0.2), -3.0, 1.5),
        "d_skip": jnp.clip(0.5 + 1.0 * jax.random.uniform(splits[9], (HEADS,), jnp.float32) ** levels(splits[9], (HEADS,), ((0, 2),), -0.2, 0.2), 0.5, 1.5),
        "gate_gain": jnp.clip(1.0 + 0.1 * jax.random.normal(splits[10], (DI,), jnp.float32), 0.5, 1.5),
        "w_out": centred(splits[11], (DI, D), DI ** -0.5, 0.09375, ((0, 2),)),
        "cotangent": centred(splits[12], (TOKENS, D), 1.0, 6.0, ((0, 16),)),
        "block_parent": draw_block_parent(jax.random.fold_in(splits[14], 71), 0),
    }


epsilon = 1e-05
highest = lax.Precision.HIGHEST

@jax.custom_vjp
def low(v):
    return lax.optimization_barrier(v.astype(jnp.bfloat16)).astype(jnp.float32)

@jax.custom_vjp
def low_back(v):
    return v

def low_keep(v):
    return (low(v), None)

def low_pass(kept, grad):
    return (grad,)

def back_keep(v):
    return (v, None)

def back_low(kept, grad):
    return (low(grad),)
low.defvjp(low_keep, low_pass)
low_back.defvjp(back_keep, back_low)

def conv_path(inputs, kernel, parent):
    blocks = parent.shape[0]
    tokens, channels = inputs.shape
    window = kernel.shape[0] - 1
    block_len = tokens // blocks
    blocked = inputs.reshape(blocks, block_len, channels)
    trailing = blocked[:, block_len - (window - 1):, :]
    context = jnp.take(trailing, jnp.maximum(parent, 0), axis=0)
    context = jnp.where((parent >= 0)[:, None, None], context, jnp.zeros_like(context))
    padded = jnp.concatenate([context, blocked], axis=1)
    summed = kernel[window][None, None, :] + jnp.zeros_like(blocked)
    for offset in range(window):
        summed = summed + kernel[offset][None, None, :] * padded[:, offset:offset + block_len, :]
    return jax.nn.silu(summed).reshape(tokens, channels)

def decay_paths(block_decay, parent):
    blocks = parent.shape[0]
    n_heads = block_decay.shape[1]
    parent_map = (parent[:, None] == jnp.arange(blocks, dtype=jnp.int32)[None, :]).astype(jnp.float32)
    identity = jnp.eye(blocks, dtype=jnp.float32)

    def advance(turn, paths):
        return identity[None] + jnp.einsum('hb,bp,hpa->hba', block_decay.T, parent_map, paths, precision=highest)
    paths = lax.fori_loop(0, blocks, advance, jnp.broadcast_to(identity, (n_heads, blocks, blocks)))
    return (paths, parent_map)

def ssd_mix(x_heads, b_rows, c_rows, dt_raw, dt_bias, a_log, d_skip, parent):
    tokens, n_heads, head_dim = x_heads.shape
    blocks = parent.shape[0]
    block_len = tokens // blocks
    dt_values = jax.nn.softplus(dt_raw + dt_bias)
    log_rate = dt_values * -jnp.exp(a_log)
    x_blocks = x_heads.reshape(blocks, block_len, n_heads, head_dim)
    b_blocks = b_rows.reshape(blocks, block_len, -1)
    c_blocks = c_rows.reshape(blocks, block_len, -1)
    dt_blocks = dt_values.reshape(blocks, block_len, n_heads)
    cumulant = jnp.cumsum(log_rate.reshape(blocks, block_len, n_heads), axis=1)
    scores = jnp.einsum('bin,bjn->bij', c_blocks, b_blocks, precision=highest)
    rows_idx = jnp.arange(block_len, dtype=jnp.int32)
    causal = (rows_idx[:, None] >= rows_idx[None, :])[None, :, :, None]
    log_gap = cumulant[:, :, None, :] - cumulant[:, None, :, :]
    decays = jnp.where(causal, jnp.exp(jnp.where(causal, log_gap, 0.0)), 0.0)
    weights = scores[..., None] * decays * dt_blocks[:, None, :, :]
    within = jnp.einsum('bijh,bjhp->bihp', weights, x_blocks, precision=highest)
    to_end = jnp.exp(cumulant[:, -1:, :] - cumulant) * dt_blocks
    local_states = jnp.einsum('bjh,bjhp,bjn->bhpn', to_end, x_blocks, b_blocks, precision=highest)
    paths, parent_map = decay_paths(jnp.exp(cumulant[:, -1, :]), parent)
    end_states = jnp.einsum('hba,ahpn->bhpn', paths, local_states, precision=highest)
    start_states = jnp.einsum('bq,qhpn->bhpn', parent_map, end_states, precision=highest)
    carried = jnp.exp(cumulant)[..., None] * jnp.einsum('bin,bhpn->bihp', c_blocks, start_states, precision=highest)
    result = within + carried + d_skip[None, None, :, None] * x_blocks
    return result.reshape(tokens, n_heads * head_dim)

def gated_mix(x_heads, bc_rows, dt_raw, dt_bias, a_log, d_skip, z_gate, parent):
    half = bc_rows.shape[1] // 2
    mixed_heads = ssd_mix(x_heads, bc_rows[:, :half], bc_rows[:, half:], dt_raw, dt_bias, a_log, d_skip, parent)
    return mixed_heads * jax.nn.silu(z_gate)

def block_layer(x_float, norm_gain, w_zx, w_bc, w_dt, conv_x, conv_bc, dt_bias, a_log, d_skip, gate_gain, w_out, parent):
    tokens = x_float.shape[0]
    n_heads = w_dt.shape[1]
    inv_rms = lax.rsqrt(lax.optimization_barrier(jnp.mean(x_float * x_float, axis=-1)) + epsilon)
    normed = low(x_float * inv_rms[:, None] * norm_gain)
    z_gate = low_back(jnp.dot(normed, w_zx[:, 0, :], precision=highest, preferred_element_type=jnp.float32))
    x_pre = low_back(jnp.dot(normed, w_zx[:, 1, :], precision=highest, preferred_element_type=jnp.float32))
    bc_pre = low_back(jnp.dot(normed, w_bc, precision=highest, preferred_element_type=jnp.float32))
    dt_raw = low_back(jnp.dot(normed, w_dt, precision=highest, preferred_element_type=jnp.float32))
    x_conv = low(conv_path(x_pre, conv_x, parent))
    bc_conv = low(conv_path(bc_pre, conv_bc, parent))
    gated = gated_mix(x_conv.reshape(tokens, n_heads, -1), bc_conv, dt_raw, dt_bias, a_log, d_skip, z_gate, parent)
    inv_gate = lax.rsqrt(lax.optimization_barrier(jnp.mean(gated * gated, axis=-1)) + epsilon)
    gate_normed = low(gated * inv_gate[:, None] * gate_gain)
    return x_float + jnp.dot(gate_normed, w_out, precision=highest, preferred_element_type=jnp.float32)

def reference(x_in, norm_gain, w_zx, w_bc, w_dt, conv_x, conv_bc, dt_bias, a_log, d_skip, gate_gain, w_out, cotangent, block_parent):
    params = (norm_gain.astype(jnp.float32), w_zx.astype(jnp.float32), w_bc.astype(jnp.float32), w_dt.astype(jnp.float32), conv_x.astype(jnp.float32), conv_bc.astype(jnp.float32), dt_bias.astype(jnp.float32), a_log.astype(jnp.float32), d_skip.astype(jnp.float32), gate_gain.astype(jnp.float32), w_out.astype(jnp.float32))

    def group(totals, item):
        x_group, cot_group, parent_group = item
        x_float = x_group.astype(jnp.float32)

        def forward(x_value, *weights):
            return block_layer(x_value, *weights, parent_group)
        result, pull = jax.vjp(forward, x_float, *params)
        grads = pull(cot_group.astype(jnp.float32))
        totals = tuple((left + right for left, right in zip(totals, grads[1:])))
        return (totals, (result.astype(jnp.bfloat16), grads[0].astype(jnp.bfloat16)))
    zeros = tuple((jnp.zeros(value.shape, jnp.float32) for value in params))
    sums, outputs = lax.scan(group, zeros, (x_in.reshape(N_DP, -1, D), cotangent.reshape(N_DP, -1, D), block_parent.reshape(N_DP, -1)))
    mixed, input_grad = outputs
    return (mixed.reshape(-1, D), input_grad.reshape(-1, D), sums[0], sums[1], sums[2], sums[3], sums[4], sums[5], sums[6], sums[7], sums[8], sums[9], sums[10])
```

```python
import functools

import jax
import jax.numpy as jnp
from jax import lax
from jax.experimental import pallas as pl
from jax.experimental.pallas import tpu as pltpu
from jax.sharding import PartitionSpec as P

epsilon = 1e-05
f32 = jnp.float32
bf16 = jnp.bfloat16
VMEM_LIMIT = 60 * 1024 * 1024
LIGHT = pl.CostEstimate(flops=1000, bytes_accessed=1000, transcendentals=0)


def sigmoid(v):
    return 0.5 * jnp.tanh(0.5 * v) + 0.5


def dot(a, b, dims=((1,), (0,)), precision=None):
    return lax.dot_general(a, b, (dims, ((), ())), precision=precision, preferred_element_type=f32)


NN = ((1,), (0,))
NT = ((1,), (1,))
TN = ((0,), (0,))
highest = lax.Precision.HIGHEST


def split_low(v):
    hi = v.astype(bf16)
    lo = (v - hi.astype(f32)).astype(bf16)
    return hi, lo


def head_masks(length, head_dim):
    lane = lax.broadcasted_iota(jnp.int32, (length, 2 * head_dim), 1)
    return lane < head_dim


def pair_stack(v, first):
    zero = jnp.zeros_like(v)
    return jnp.concatenate([jnp.where(first, v, zero), jnp.where(first, zero, v)], axis=0)


def tri_mask(length):
    row = lax.broadcasted_iota(jnp.int32, (length, length), 0)
    col = lax.broadcasted_iota(jnp.int32, (length, length), 1)
    return row, col


def step_values(dtr_ref, bias_ref, alog_ref, length):
    row, col = tri_mask(length)
    dtr = dtr_ref[...] + bias_ref[...]
    dt = jnp.maximum(dtr, 0.0) + jnp.log1p(jnp.exp(-jnp.abs(dtr)))
    rate = -jnp.exp(alog_ref[...])
    tri = (row >= col).astype(f32)
    cum = dot(tri, dt * rate, NN, highest)
    last = cum[length - 1 : length, :]
    return dtr, dt, rate, cum, jnp.exp(cum), jnp.exp(jnp.minimum(last - cum, 0.0))


def store_columns(cum, cum_s, cumt_s, heads):
    cum_s[:, :heads] = cum
    cumt_s[...] = jnp.transpose(cum_s[...])


def conv_rows(ext, kern, length, window):
    base = ext.shape[0] - length - (window - 1)
    total = kern[window : window + 1, :] + kern[window - 1 : window, :] * ext[ext.shape[0] - length :, :]
    for offset in range(window - 1):
        total = total + kern[offset : offset + 1, :] * ext[base + offset : base + offset + length, :]
    return total


def forward_kernel(
    sizes,
    par_ref,
    bc_ref,
    dtr_ref,
    z_ref,
    xp_ref,
    kx_ref,
    kbc_ref,
    bias_ref,
    alog_ref,
    skip_ref,
    gain_ref,
    sel_ref,
    y_ref,
    xc_ref,
    pre_ref,
    gg_ref,
    bcc_ref,
    bcp_ref,
    hs_ref,
    sq_ref,
    h_end,
    tail_x,
    tail_bc,
    lhs_s,
    cum_s,
    cumt_s,
    score_s,
    acc_s,
):
    length, inner, heads, head_dim, lanes, blocks, window = sizes
    state = bcc_ref.shape[1] // 2
    b = pl.program_id(0)
    par = par_ref[b]
    slot = jnp.where(par >= 0, par, blocks)

    @pl.when(b == 0)
    def _():
        h_end[blocks] = jnp.zeros(h_end.shape[1:], f32)
        tail_x[blocks] = jnp.zeros(tail_x.shape[1:], f32)
        tail_bc[blocks] = jnp.zeros(tail_bc.shape[1:], f32)
        cum_s[...] = jnp.zeros_like(cum_s)

    bcv = bc_ref[...]
    pre = conv_rows(jnp.concatenate([tail_bc[slot], bcv], axis=0), kbc_ref[...], length, window)
    tail_bc[b] = bcv[length - 8 :, :]
    bcc = (pre * sigmoid(pre)).astype(bf16)
    bcc_ref[...] = bcc
    bcp_ref[...] = pre
    c_rows = bcc[:, state:]
    b_rows = bcc[:, :state]
    row, col = tri_mask(length)
    score_s[...] = jnp.where(row >= col, dot(c_rows, b_rows, NT), 0.0)

    _, dt, _, cum, from_start, to_end = step_values(dtr_ref, bias_ref, alog_ref, length)
    hi, lo = split_low(jnp.concatenate([dt, from_start, to_end], axis=0))
    lhs_s[...] = jnp.concatenate([hi, lo], axis=1)
    store_columns(cum, cum_s, cumt_s, heads)
    acc_s[...] = jnp.zeros_like(acc_s)
    first = head_masks(length, head_dim)
    group = lanes // head_dim
    pair = 2 * head_dim

    def body(g, carry):
        sl = pl.ds(pl.multiple_of(g * lanes, lanes), lanes)
        xpv = xp_ref[:, sl].astype(f32)
        ext = jnp.concatenate([tail_x[slot, :, sl], xpv], axis=0)
        pre_x = conv_rows(ext, kx_ref[:, sl], length, window)
        tail_x[b, :, sl] = xpv[length - 8 :, :]
        xc = (pre_x * sigmoid(pre_x)).astype(bf16)
        pre_ref[:, sl] = pre_x.astype(bf16)
        xc_ref[:, sl] = xc
        wide = dot(lhs_s[...], sel_ref[:, sl])
        dt_l = wide[:length]
        start_l = wide[length : 2 * length]
        end_l = wide[2 * length :]
        xcf = xc.astype(f32)
        xd = dt_l * xcf
        xdb = xd.astype(bf16)
        gx = (end_l * xd).astype(bf16)
        h = h_end[slot, :, sl]
        hb = h.astype(bf16)
        hs_ref[0, :, sl] = hb
        carried = start_l * dot(c_rows, hb)
        h_end[b, :, sl] = start_l[length - 1 : length, :] * h + dot(b_rows, gx, TN)
        cols = pltpu.roll(cum_s[...], cum_s.shape[1] - g * group, 1)
        rows = cumt_s[pl.ds(pl.multiple_of(g * group, 8), max(group, 8)), :]
        score = score_s[...]
        skip = skip_ref[:, sl]
        gain = gain_ref[:, sl]
        zv = z_ref[:, sl].astype(f32)
        gate = zv * sigmoid(zv)
        acc = acc_s[...]
        for q in range(lanes // pair):
            at = slice(q * pair, (q + 1) * pair)
            weights = []
            for h_at in (2 * q, 2 * q + 1):
                gap = jnp.minimum(cols[:, h_at : h_at + 1] - rows[h_at : h_at + 1, :], 0.0)
                weights.append((score * jnp.exp(gap)).astype(bf16))
            within = dot(jnp.concatenate(weights, axis=1), pair_stack(xdb[:, at], first))
            y = (within + carried[:, at] + skip[:, at] * xcf[:, at]).astype(bf16)
            out = pl.ds(pl.multiple_of(g * lanes + q * pair, pair), pair)
            y_ref[:, out] = y
            gated = y.astype(f32) * gate[:, at]
            gained = gated * gain[:, at]
            gg_ref[:, out] = gained.astype(bf16)
            acc = acc + gated * gated
        acc_s[...] = acc
        return carry

    lax.fori_loop(0, inner // lanes, body, 0)
    sq_ref[0] = dot(jnp.ones((8, pair), f32), acc_s[...], NT, highest)


def run_forward(parent, bc_pre, dt_raw, zx, conv_x, conv_bc, dt_bias, a_log, skip_l, gate_gain, sel):
    tokens = zx.shape[0]
    inner = conv_x.shape[1]
    heads = dt_raw.shape[1]
    head_dim = inner // heads
    blocks = parent.shape[0]
    length = tokens // blocks
    window = conv_x.shape[0] - 1
    wide = bc_pre.shape[1]
    state = wide // 2
    lanes = min(512, inner)
    sizes = (length, inner, heads, head_dim, lanes, blocks, window)
    whole = lambda shape: pl.BlockSpec(shape, lambda b, *_: (0,) * len(shape))
    rows = lambda width: pl.BlockSpec((length, width), lambda b, *_: (b, 0))
    block = lambda shape: pl.BlockSpec((1,) + shape, lambda b, *_: (b, 0, 0))
    grid_spec = pltpu.PrefetchScalarGridSpec(
        num_scalar_prefetch=1,
        grid=(blocks,),
        in_specs=[
            rows(wide),
            rows(heads),
            rows(inner),
            pl.BlockSpec((length, inner), lambda b, *_: (b, 1)),
            whole(conv_x.shape),
            whole(conv_bc.shape),
            whole((1, heads)),
            whole((1, heads)),
            whole((1, inner)),
            whole((1, inner)),
            whole(sel.shape),
        ],
        out_specs=[
            rows(inner),
            rows(inner),
            rows(inner),
            rows(inner),
            rows(wide),
            rows(wide),
            block((state, inner)),
            block((8, length)),
        ],
        scratch_shapes=[
            pltpu.VMEM((blocks + 1, state, inner), f32),
            pltpu.VMEM((blocks + 1, 8, inner), f32),
            pltpu.VMEM((blocks + 1, 8, wide), f32),
            pltpu.VMEM((3 * length, 2 * heads), bf16),
            pltpu.VMEM((length, length), f32),
            pltpu.VMEM((length, length), f32),
            pltpu.VMEM((length, length), f32),
            pltpu.VMEM((length, 2 * head_dim), f32),
        ],
    )
    return pl.pallas_call(
        functools.partial(forward_kernel, sizes),
        grid_spec=grid_spec,
        out_shape=[jax.ShapeDtypeStruct((tokens, inner), bf16)] * 4
        + [
            jax.ShapeDtypeStruct((tokens, wide), bf16),
            jax.ShapeDtypeStruct((tokens, wide), f32),
            jax.ShapeDtypeStruct((blocks, state, inner), bf16),
            jax.ShapeDtypeStruct((blocks, 8, length), f32),
        ],
        compiler_params=pltpu.CompilerParams(vmem_limit_bytes=VMEM_LIMIT),
        cost_estimate=LIGHT,
        name="ssd_forward",
    )(parent, bc_pre, dt_raw, zx, zx, conv_x, conv_bc, dt_bias[None], a_log[None], skip_l, gate_gain[None], sel)


def token_column(row_ref, at, length):
    row = row_ref[pl.ds(at, 1), :]
    return jnp.transpose(jnp.broadcast_to(row, (length, length)))


def ungate_kernel(sizes, sq_ref, cross_ref, y_ref, z_ref, dgn_ref, gain_ref, dz_ref, dy_ref, grad_ref):
    length, inner, lanes, full = sizes
    b = pl.program_id(0)
    inv = lax.rsqrt(token_column(sq_ref, b, length) / full + epsilon)
    coef = inv * token_column(cross_ref, b, length) / full

    @pl.when(b == 0)
    def _():
        grad_ref[...] = jnp.zeros_like(grad_ref)

    def body(g, carry):
        sl = pl.ds(pl.multiple_of(g * length, length), length)
        zv = z_ref[:, sl].astype(f32)
        sig = sigmoid(zv)
        gate = zv * sig
        gain = gain_ref[:, sl]
        y = y_ref[:, sl].astype(f32) * inv
        scaled = y * gate
        dgn = dgn_ref[:, sl].astype(f32)
        grad_ref[:, sl] += jnp.sum(dgn * scaled, axis=0, keepdims=True)
        d_scaled = dgn * gain - scaled * coef
        dz_ref[:, sl] = (d_scaled * y * (sig + gate * (1.0 - sig))).astype(bf16)
        dy_ref[:, sl] = (d_scaled * inv * gate).astype(bf16)
        return carry

    lax.fori_loop(0, inner // length, body, 0, unroll=2)


def run_ungate(squares, cross, y, zx, dgn, gate_gain, full):
    tokens, inner = y.shape
    blocks, length = squares.shape
    rows = pl.BlockSpec((length, inner), lambda b: (b, 0))
    one = pl.BlockSpec((1, inner), lambda b: (0, 0))
    small = pl.BlockSpec((blocks, length), lambda b: (0, 0))
    return pl.pallas_call(
        functools.partial(ungate_kernel, (length, inner, length, full)),
        grid=(blocks,),
        in_specs=[small, small, rows, rows, rows, one],
        out_specs=[rows, rows, one],
        out_shape=[jax.ShapeDtypeStruct((tokens, inner), bf16)] * 2 + [jax.ShapeDtypeStruct((1, inner), f32)],
        compiler_params=pltpu.CompilerParams(vmem_limit_bytes=VMEM_LIMIT),
        cost_estimate=LIGHT,
        name="gate_backward",
    )(squares, cross, y, zx, dgn, gate_gain[None])


def output_kernel(left_ref, right_ref, cot_ref, out_ref, cross_ref):
    total = dot(left_ref[...], right_ref[...])
    product = (total * cot_ref[...].astype(f32)).astype(bf16)
    row = dot(jnp.ones((8, product.shape[1]), bf16), product, NT)

    @pl.when(pl.program_id(0) == 0)
    def _():
        cross_ref[...] = jnp.zeros_like(cross_ref)

    cross_ref[...] += row
    out_ref[...] = total.astype(bf16)


def run_output(gained, w_out, cotangent):
    tokens, inner = gained.shape
    features = w_out.shape[1]
    tile = min(512, features)
    return pl.pallas_call(
        output_kernel,
        grid=(features // tile,),
        in_specs=[
            pl.BlockSpec((tokens, inner), lambda j: (0, 0), pipeline_mode=pl.Buffered(1)),
            pl.BlockSpec((inner, tile), lambda j: (0, j)),
            pl.BlockSpec((tokens, tile), lambda j: (0, j)),
        ],
        out_specs=[pl.BlockSpec((tokens, tile), lambda j: (0, j)), pl.BlockSpec((8, tokens), lambda j: (0, 0))],
        out_shape=[
            jax.ShapeDtypeStruct((tokens, features), bf16),
            jax.ShapeDtypeStruct((8, tokens), f32),
        ],
        compiler_params=pltpu.CompilerParams(vmem_limit_bytes=VMEM_LIMIT),
        cost_estimate=LIGHT,
        name="output_project",
    )(gained, w_out, cotangent)


def norm_kernel(features, x_ref, cot_ref, gain_ref, wbc_ref, wdt_ref, normed_ref, turned_ref, inv_ref, bc_ref, dtr_ref):
    x = x_ref[...].astype(f32)
    inv = lax.rsqrt(jnp.sum(x * x, axis=1, keepdims=True) / features + epsilon)
    inv_ref[...] = inv
    normed = (x * inv * gain_ref[...]).astype(bf16)
    normed_ref[...] = normed
    turned_ref[0] = jnp.transpose(normed)
    turned_ref[1] = jnp.transpose(cot_ref[...])
    bc_ref[...] = dot(normed, wbc_ref[...])
    dtr_ref[...] = dot(normed, wdt_ref[...], NT)


def run_norm(x_in, cotangent, norm_gain, w_bc, w_dt_t, length):
    tokens, features = x_in.shape
    wide = w_bc.shape[1]
    heads = w_dt_t.shape[0]
    rows = lambda width: pl.BlockSpec((length, width), lambda b: (b, 0))
    whole = lambda shape: pl.BlockSpec(shape, lambda b: (0, 0), pipeline_mode=pl.Buffered(1))
    turned = pl.BlockSpec((2, features, length), lambda b: (0, 0, b))
    return pl.pallas_call(
        functools.partial(norm_kernel, features),
        grid=(tokens // length,),
        in_specs=[rows(features), rows(features), whole((1, features)), whole(w_bc.shape), whole(w_dt_t.shape)],
        out_specs=[rows(features), turned, rows(1), rows(wide), rows(heads)],
        out_shape=[
            jax.ShapeDtypeStruct((tokens, features), bf16),
            jax.ShapeDtypeStruct((2, features, tokens), bf16),
            jax.ShapeDtypeStruct((tokens, 1), f32),
            jax.ShapeDtypeStruct((tokens, wide), f32),
            jax.ShapeDtypeStruct((tokens, heads), f32),
        ],
        compiler_params=pltpu.CompilerParams(vmem_limit_bytes=VMEM_LIMIT),
        cost_estimate=LIGHT,
        name="input_norm",
    )(x_in, cotangent, norm_gain[None], w_bc, w_dt_t)


def fetch_left(share, which, place_ref, mine_ref, theirs_ref, left_s, sem):
    tokens = mine_ref.shape[2]
    count = left_s.shape[0] // share
    copies = []
    for i in range(count):
        src = pl.ds(pl.multiple_of(place_ref[i] * share, share), share)
        for side, ref in enumerate((mine_ref, theirs_ref)):
            copies.append(
                pltpu.make_async_copy(
                    ref.at[which, src, :],
                    left_s.at[pl.ds(i * share, share), pl.ds(side * tokens, tokens)],
                    sem.at[2 * i + side],
                )
            )
    return copies


def gather_right(refs, right_s):
    at = 0
    for ref in refs:
        size = ref.shape[0]
        right_s[at : at + size, :] = ref[...]
        at += size


def load_left(share, which, place_ref, mine_ref, theirs_ref, left_s, sem):
    copies = fetch_left(share, which, place_ref, mine_ref, theirs_ref, left_s, sem)
    for copy in copies:
        copy.start()
    for copy in copies:
        copy.wait()


def grad_kernel(share, which, pieces, scaled, outs, place_ref, mine_ref, theirs_ref, *rest):
    rights = rest[:pieces]
    rest = rest[pieces:]
    if scaled:
        scale_ref = rest[0]
        rest = rest[1:]
    out_refs = rest[:outs]
    left_s, right_s, sem = rest[outs:]

    @pl.when(pl.program_id(0) == 0)
    def _():
        load_left(share, which, place_ref, mine_ref, theirs_ref, left_s, sem)
        if scaled:
            rows_at = left_s.shape[0] // 8

            def apply(i, carry):
                at = pl.ds(pl.multiple_of(i * rows_at, rows_at), rows_at)
                left_s[at, :] = (left_s[at, :].astype(f32) * scale_ref[...]).astype(bf16)
                return carry

            lax.fori_loop(0, 8, apply, 0)

    gather_right(rights, right_s)
    total = dot(left_s[...], right_s[...])
    size = out_refs[0].shape[0]
    for i, ref in enumerate(out_refs):
        ref[...] = total[i * size : (i + 1) * size].astype(bf16)


def run_grad(places, which, mine, theirs, rights, share, first, width, outs, scale=None):
    tokens = mine.shape[2]
    count = places.shape[0]
    rows = count * share
    tile = 256 if width % 256 == 0 and first % 256 == 0 else 128
    anywhere = pl.BlockSpec(memory_space=pl.ANY)
    columns = [
        pl.BlockSpec((right.shape[0], tile), lambda j, *_: (0, first // tile + j)) for right in rights
    ]
    extra = [] if scale is None else [pl.BlockSpec(scale.shape, lambda j, *_: (0, 0))]
    return pl.pallas_call(
        functools.partial(grad_kernel, share, which, len(rights), scale is not None, outs),
        grid_spec=pltpu.PrefetchScalarGridSpec(
            num_scalar_prefetch=1,
            grid=(width // tile,),
            in_specs=[anywhere, anywhere] + columns + extra,
            out_specs=[pl.BlockSpec((rows // outs, tile), lambda j, *_: (0, j))] * outs,
            scratch_shapes=[
                pltpu.VMEM((rows, 2 * tokens), bf16),
                pltpu.VMEM((2 * tokens, tile), bf16),
                pltpu.SemaphoreType.DMA((2 * count,)),
            ],
        ),
        out_shape=[jax.ShapeDtypeStruct((rows // outs, width), bf16)] * outs,
        compiler_params=pltpu.CompilerParams(vmem_limit_bytes=VMEM_LIMIT),
        cost_estimate=LIGHT,
        name="weight_grad",
    )(places, mine, theirs, *rights, *([] if scale is None else [scale]))


def input_kernel(heads, dz_ref, dx_ref, dbc_ref, ddt_ref, wz_ref, wx_ref, wbc_ref, wdt_ref, x_ref, inv_ref, out_ref, gain_ref):
    total = dot(dz_ref[...], wz_ref[...], NT) + dot(dx_ref[...], wx_ref[...], NT)
    total = total + dot(dbc_ref[...], wbc_ref[...], NT)
    total = total + dot(ddt_ref[:, :heads], wdt_ref[...], NN)
    out_ref[...] = total.astype(bf16)
    gain_ref[...] = jnp.sum(total * (x_ref[...].astype(f32) * inv_ref[...]), axis=0, keepdims=True)


def run_input(dz, dx, dbc, ddt, w_cat, w_bc, w_dt_t, x_in, inv_rms, at, tokens):
    inner = dz.shape[1]
    features = x_in.shape[1]
    wide = w_bc.shape[1]
    heads = w_dt_t.shape[0]
    tile = 256
    side = lambda width: pl.BlockSpec((tokens, width), lambda j: (at, 0), pipeline_mode=pl.Buffered(1))
    return pl.pallas_call(
        functools.partial(input_kernel, heads),
        grid=(features // tile,),
        in_specs=[
            side(inner),
            side(inner),
            side(wide),
            side(ddt.shape[1]),
            pl.BlockSpec((tile, inner), lambda j: (j, 0)),
            pl.BlockSpec((tile, inner), lambda j: (j, 1)),
            pl.BlockSpec((tile, wide), lambda j: (j, 0)),
            pl.BlockSpec((heads, tile), lambda j: (0, j)),
            pl.BlockSpec((tokens, tile), lambda j: (at, j)),
            pl.BlockSpec((tokens, 1), lambda j: (at, 0)),
        ],
        out_specs=[pl.BlockSpec((tokens, tile), lambda j: (0, j)), pl.BlockSpec((1, tile), lambda j: (0, j))],
        out_shape=[jax.ShapeDtypeStruct((tokens, features), bf16), jax.ShapeDtypeStruct((1, features), f32)],
        compiler_params=pltpu.CompilerParams(vmem_limit_bytes=VMEM_LIMIT),
        cost_estimate=LIGHT,
        name="input_grad",
    )(dz, dx, dbc, ddt, w_cat, w_cat, w_bc, w_dt_t, x_in, inv_rms)


def conv_back(ext, kern, inputs, length, window):
    total = kern[window - 1 : window, :] * ext[:length, :]
    sums = [None] * (window + 1)
    sums[window] = jnp.sum(ext[:length, :], axis=0, keepdims=True)
    sums[window - 1] = jnp.sum(inputs * ext[:length, :], axis=0, keepdims=True)
    for shift in range(1, window):
        moved = ext[shift : shift + length, :]
        total = total + kern[window - 1 - shift : window - shift, :] * moved
        sums[window - 1 - shift] = jnp.sum(inputs * moved, axis=0, keepdims=True)
    return total, jnp.concatenate(sums, axis=0)


def backward_kernel(
    sizes,
    par_ref,
    dy_ref,
    xc_ref,
    pre_ref,
    xp_ref,
    hs_ref,
    bcc_ref,
    bcp_ref,
    bc_ref,
    dtr_ref,
    kx_ref,
    kbc_ref,
    bias_ref,
    alog_ref,
    skip_ref,
    sel_ref,
    selt_ref,
    *rest,
):
    length, inner, heads, head_dim, lanes, blocks, window, start, count = sizes
    last_chunk = start + count == blocks
    if not last_chunk:
        ds_prev, nx_prev, nbc_prev = rest[:3]
        rest = rest[3:]
    dxp_ref, dbc_ref, ddt_ref, gkx_ref, gkbc_ref, gskip_ref, ghead_ref = rest[:7]
    rest = rest[7:]
    if start:
        ds_next, nx_next, nbc_next = rest[:3]
        rest = rest[3:]
    (
        d_state,
        next_x,
        next_bc,
        lhs_s,
        cum_s,
        cumt_s,
        score_s,
        dscore_s,
        db_s,
        dc_s,
        red_s,
        cross_s,
        inner_s,
    ) = rest
    state = bcc_ref.shape[1] // 2
    b = start + count - 1 - pl.program_id(0)
    par = par_ref[b]
    slot = jnp.where(par >= 0, par, blocks)

    @pl.when(pl.program_id(0) == 0)
    def _():
        if last_chunk:
            d_state[...] = jnp.zeros_like(d_state)
            next_x[...] = jnp.zeros_like(next_x)
            next_bc[...] = jnp.zeros_like(next_bc)
        else:
            pltpu.sync_copy(ds_prev, d_state.at[: start + count])
            next_x[: start + count] = nx_prev[...]
            next_bc[: start + count] = nbc_prev[...]
            d_state[blocks] = jnp.zeros(d_state.shape[1:], f32)
            next_x[blocks] = jnp.zeros(next_x.shape[1:], f32)
            next_bc[blocks] = jnp.zeros(next_bc.shape[1:], f32)
        cum_s[...] = jnp.zeros_like(cum_s)
        cross_s[...] = jnp.zeros_like(cross_s)
        gkx_ref[...] = jnp.zeros_like(gkx_ref)
        gkbc_ref[...] = jnp.zeros_like(gkbc_ref)
        gskip_ref[...] = jnp.zeros_like(gskip_ref)
        ghead_ref[...] = jnp.zeros_like(ghead_ref)

    bcc = bcc_ref[...]
    c_rows = bcc[:, state:]
    b_rows = bcc[:, :state]
    row, col = tri_mask(length)
    score_s[...] = jnp.where(row >= col, dot(c_rows, b_rows, NT), 0.0)
    dtr, dt, rate, cum, from_start, to_end = step_values(dtr_ref, bias_ref, alog_ref, length)
    hi, lo = split_low(jnp.concatenate([dt, from_start, to_end], axis=0))
    lhs_s[...] = jnp.concatenate([hi, lo], axis=1)
    store_columns(cum, cum_s, cumt_s, heads)
    dscore_s[...] = jnp.zeros_like(dscore_s)
    db_s[...] = jnp.zeros_like(db_s)
    dc_s[...] = jnp.zeros_like(dc_s)
    red_s[...] = jnp.zeros_like(red_s)
    first = head_masks(length, head_dim)
    group = lanes // head_dim
    pair = 2 * head_dim
    before = (row < col).astype(bf16)
    following = (row >= col).astype(f32)

    def body(g, carry):
        sl = pl.ds(pl.multiple_of(g * lanes, lanes), lanes)
        wide = dot(lhs_s[...], sel_ref[:, sl])
        dt_l = wide[:length]
        start_l = wide[length : 2 * length]
        end_l = wide[2 * length :]
        last_l = start_l[length - 1 : length, :]
        dyb = dy_ref[:, sl]
        dy = dyb.astype(f32)
        xc = xc_ref[:, sl]
        xcf = xc.astype(f32)
        xd = dt_l * xcf
        xdb = xd.astype(bf16)
        gx = (end_l * xd).astype(bf16)
        hb = hs_ref[0, :, sl]
        d_end = d_state[b, :, sl]
        d_endb = d_end.astype(bf16)
        sdy = (start_l * dy).astype(bf16)
        carried = start_l * dot(c_rows, hb)
        local = end_l * dot(b_rows, d_endb)
        dc_s[...] += dot(sdy, hb, NT)
        db_s[...] += dot(gx, d_endb, NT)
        d_state[slot, :, sl] += last_l * d_end + dot(c_rows, sdy, TN)
        carry_end = jnp.sum(d_end * hb.astype(f32), axis=0, keepdims=True) * last_l
        cols = pltpu.roll(cum_s[...], cum_s.shape[1] - g * group, 1)
        rows = cumt_s[pl.ds(pl.multiple_of(g * group, 8), max(group, 8)), :]
        score = score_s[...]
        dscore = dscore_s[...]
        crossings = []
        for q in range(lanes // pair):
            at = slice(q * pair, (q + 1) * pair)
            dy2 = pair_stack(dyb[:, at], first)
            dw2 = dot(dy2, xdb[:, at], NT)
            weights, terms = [], []
            for half in range(2):
                h_at = 2 * q + half
                gap = jnp.minimum(cols[:, h_at : h_at + 1] - rows[h_at : h_at + 1, :], 0.0)
                decay = jnp.exp(gap)
                weights.append((score * decay).astype(bf16))
                t = dw2[half * length : (half + 1) * length] * decay
                dscore = dscore + t
                terms.append((t * score).astype(bf16))
            inner_s[:, at] = dot(jnp.concatenate(weights, axis=0), dy2, TN)
            crossed = dot(jnp.concatenate(terms, axis=0), before)
            for half in range(2):
                part = crossed[half * length : (half + 1) * length] * following
                crossings.append(jnp.sum(part, axis=0, keepdims=True))
        dscore_s[...] = dscore
        cross_s[pl.ds(pl.multiple_of(g * group, 8), group), :] = jnp.concatenate(crossings, axis=0)
        dxd = inner_s[...] + local
        products = jnp.concatenate(
            [(dy * carried).astype(bf16), (local * xd).astype(bf16), (dxd * xcf).astype(bf16),
             jnp.broadcast_to(carry_end, (16, lanes)).astype(bf16)], axis=0
        )
        red_s[...] += dot(products, selt_ref[sl, :])
        gskip_ref[:, sl] += jnp.sum(dy * xcf, axis=0, keepdims=True)
        dx = dt_l * dxd + skip_ref[:, sl] * dy
        pre = pre_ref[:, sl].astype(f32)
        sig = sigmoid(pre)
        d_pre = dx * (sig + pre * sig * (1.0 - sig))
        ext = jnp.concatenate([d_pre, next_x[b, :, sl]], axis=0)
        next_x[slot, :, sl] += d_pre[:8, :]
        xpv = xp_ref[:, sl].astype(f32)
        dxp, sums = conv_back(ext, kx_ref[:, sl], xpv, length, window)
        dxp_ref[:, sl] = dxp.astype(bf16)
        gkx_ref[:, sl] += sums
        return carry

    lax.fori_loop(0, inner // lanes, body, 0)

    red = red_s[...]
    carried_t = red[:length, :heads]
    local_t = red[length : 2 * length, :heads]
    ddt = red[2 * length : 3 * length, :heads]
    end_t = red[3 * length : 3 * length + 1, :heads]
    suffix = (row <= col).astype(f32)
    prefix = (row > col).astype(f32)
    d_rate = (
        dot(suffix, carried_t, NN, highest)
        + dot(prefix, local_t, NN, highest)
        + end_t
        + jnp.transpose(cross_s[...])[:, :heads]
    )
    ddt = ddt + d_rate * rate
    ddtr = ddt * sigmoid(dtr)
    ghead_ref[0:1, :] += jnp.sum(ddtr, axis=0, keepdims=True)
    ghead_ref[1:2, :] += jnp.sum(d_rate * rate * dt, axis=0, keepdims=True)

    dscore = jnp.where(row >= col, dscore_s[...], 0.0).astype(bf16)
    d_c = dc_s[...] + dot(dscore, b_rows)
    d_b = db_s[...] + dot(dscore, c_rows, TN)
    pre = bcp_ref[...]
    sig = sigmoid(pre)
    d_pre = jnp.concatenate([d_b, d_c], axis=1) * (sig + pre * sig * (1.0 - sig))
    ext = jnp.concatenate([d_pre, next_bc[b]], axis=0)
    next_bc[slot] += d_pre[:8, :]
    dbcp, sums = conv_back(ext, kbc_ref[...], bc_ref[...], length, window)
    gkbc_ref[...] += sums
    dbc_ref[...] = dbcp.astype(bf16)
    ddt_ref[...] = jnp.zeros_like(ddt_ref)
    ddt_ref[:, :heads] = ddtr.astype(bf16)

    if start:

        @pl.when(b == start)
        def _():
            pltpu.sync_copy(d_state.at[:start], ds_next)
            nx_next[...] = next_x[:start]
            nbc_next[...] = next_bc[:start]


def run_backward(
    start, count, parent, dy, xc, pre, zx, hs, bcc, bcp, bc_pre, dt_raw, conv_x, conv_bc, dt_bias, a_log, skip_l,
    sel, sel_t, small, carry
):
    inner = conv_x.shape[1]
    heads = dt_raw.shape[1]
    head_dim = inner // heads
    blocks = parent.shape[0]
    length = dy.shape[0] // blocks
    tokens = count * length
    window = conv_x.shape[0] - 1
    wide = bcc.shape[1]
    state = wide // 2
    lanes = min(512, inner)
    anywhere = pl.BlockSpec(memory_space=pl.ANY)
    sizes = (length, inner, heads, head_dim, lanes, blocks, window, start, count)
    top = count - 1
    later = lambda width: pl.BlockSpec((length, width), lambda b, *_: (start + top - b, 0))
    whole = lambda shape: pl.BlockSpec(shape, lambda b, *_: (0,) * len(shape))
    rows = lambda width: pl.BlockSpec((length, width), lambda b, *_: (top - b, 0))
    carry_specs = [anywhere, whole(carry[1].shape), whole(carry[2].shape)] if carry else []
    next_specs, next_shapes = [], []
    if start:
        shapes = [(start, state, inner), (start, 8, inner), (start, 8, wide)]
        next_specs = [anywhere, whole(shapes[1]), whole(shapes[2])]
        next_shapes = [jax.ShapeDtypeStruct(shape, f32) for shape in shapes]
    grid_spec = pltpu.PrefetchScalarGridSpec(
        num_scalar_prefetch=1,
        grid=(count,),
        in_specs=[
            later(inner),
            later(inner),
            later(inner),
            pl.BlockSpec((length, inner), lambda b, *_: (start + top - b, 1)),
            pl.BlockSpec((1, state, inner), lambda b, *_: (start + top - b, 0, 0)),
            later(wide),
            later(wide),
            later(wide),
            later(heads),
            whole(conv_x.shape),
            whole(conv_bc.shape),
            whole((1, heads)),
            whole((1, heads)),
            whole((1, inner)),
            whole(sel.shape),
            whole(sel_t.shape),
        ]
        + carry_specs,
        out_specs=[
            rows(inner),
            rows(wide),
            rows(small - wide),
            whole(conv_x.shape),
            whole(conv_bc.shape),
            whole((1, inner)),
            whole((2, heads)),
        ]
        + next_specs,
        scratch_shapes=[
            pltpu.VMEM((blocks + 1, state, inner), f32),
            pltpu.VMEM((blocks + 1, 8, inner), f32),
            pltpu.VMEM((blocks + 1, 8, wide), f32),
            pltpu.VMEM((3 * length, 2 * heads), bf16),
            pltpu.VMEM((length, length), f32),
            pltpu.VMEM((length, length), f32),
            pltpu.VMEM((length, length), f32),
            pltpu.VMEM((length, length), f32),
            pltpu.VMEM((length, state), f32),
            pltpu.VMEM((length, state), f32),
            pltpu.VMEM((3 * length + 16, sel_t.shape[1]), f32),
            pltpu.VMEM((length, length), f32),
            pltpu.VMEM((length, lanes), f32),
        ],
    )
    return pl.pallas_call(
        functools.partial(backward_kernel, sizes),
        grid_spec=grid_spec,
        out_shape=[
            jax.ShapeDtypeStruct((tokens, inner), bf16),
            jax.ShapeDtypeStruct((tokens, wide), bf16),
            jax.ShapeDtypeStruct((tokens, small - wide), bf16),
            jax.ShapeDtypeStruct(conv_x.shape, f32),
            jax.ShapeDtypeStruct(conv_bc.shape, f32),
            jax.ShapeDtypeStruct((1, inner), f32),
            jax.ShapeDtypeStruct((2, heads), f32),
        ]
        + next_shapes,
        compiler_params=pltpu.CompilerParams(vmem_limit_bytes=VMEM_LIMIT),
        cost_estimate=LIGHT,
        name="ssd_backward",
    )(
        parent, dy, xc, pre, zx, hs, bcc, bcp, bc_pre, dt_raw, conv_x, conv_bc,
        dt_bias[None], a_log[None], skip_l, sel, sel_t, *carry,
    )


def add_kernel(terms, *refs):
    out_refs = refs[terms:]
    size = out_refs[0].shape[0]
    for i, out in enumerate(out_refs):
        rows = slice(i * size, (i + 1) * size)
        total = refs[0][rows, :].astype(f32)
        for ref in refs[1:terms]:
            total = total + ref[rows, :].astype(f32)
        out[...] = total.astype(out.dtype)


def run_add(values, pieces, kind):
    rows, width = values[0].shape
    tile = width // 2 if rows * width > 65536 and width % 256 == 0 else width
    spec = lambda size: pl.BlockSpec((size, tile), lambda j: (0, j))
    size = rows // pieces
    return pl.pallas_call(
        functools.partial(add_kernel, len(values)),
        grid=(width // tile,),
        in_specs=[spec(rows)] * len(values),
        out_specs=[spec(size)] * pieces,
        out_shape=[jax.ShapeDtypeStruct((size, width), kind)] * pieces,
        compiler_params=pltpu.CompilerParams(vmem_limit_bytes=VMEM_LIMIT),
        cost_estimate=LIGHT,
        name="add_parts",
    )(*values)


def mixed_kernel(full, terms, sq_ref, x_ref, *refs):
    length = x_ref.shape[0]
    inv = lax.rsqrt(token_column(sq_ref, pl.program_id(0), length)[:, :1] / full + epsilon)
    total = refs[0][...].astype(f32)
    for ref in refs[1:terms]:
        total = total + ref[...].astype(f32)
    refs[terms][...] = (x_ref[...].astype(f32) + inv * total).astype(bf16)


def run_mixed(squares, x_in, values, full):
    tokens, features = x_in.shape
    blocks, length = squares.shape
    rows = pl.BlockSpec((length, features), lambda b: (b, 0))
    return pl.pallas_call(
        functools.partial(mixed_kernel, full, len(values)),
        grid=(blocks,),
        in_specs=[pl.BlockSpec((blocks, length), lambda b: (0, 0)), rows] + [rows] * len(values),
        out_specs=rows,
        out_shape=jax.ShapeDtypeStruct((tokens, features), bf16),
        compiler_params=pltpu.CompilerParams(vmem_limit_bytes=VMEM_LIMIT),
        cost_estimate=LIGHT,
        name="layer_output",
    )(squares, x_in, *values)


def finish_kernel(terms, x_ref, cot_ref, inv_ref, gain_ref, *refs):
    x = x_ref[...].astype(f32)
    inv = inv_ref[...]
    total = refs[0][...].astype(f32)
    for ref in refs[1:terms]:
        total = total + ref[...].astype(f32)
    gained = total * gain_ref[...]
    spread = inv * inv * inv * jnp.sum(gained * x, axis=1, keepdims=True) / x.shape[1]
    refs[-1][...] = (cot_ref[...].astype(f32) + inv * gained - x * spread).astype(bf16)


def run_finish(values, x_in, cotangent, inv_rms, norm_gain, first, length, into):
    tokens, features = x_in.shape
    count = values[0].shape[0] // length
    later = lambda width: pl.BlockSpec((length, width), lambda b: (first + b, 0))
    rows = pl.BlockSpec((length, features), lambda b: (b, 0))
    extra = [] if into is None else [into]
    return pl.pallas_call(
        functools.partial(finish_kernel, len(values)),
        grid=(count,),
        in_specs=[later(features), later(features), later(1), pl.BlockSpec((1, features), lambda b: (0, 0))]
        + [rows] * len(values)
        + [pl.BlockSpec(memory_space=pl.ANY)] * len(extra),
        out_specs=later(features),
        out_shape=jax.ShapeDtypeStruct((tokens, features), bf16),
        input_output_aliases={} if into is None else {4 + len(values): 0},
        compiler_params=pltpu.CompilerParams(vmem_limit_bytes=VMEM_LIMIT),
        cost_estimate=LIGHT,
        name="input_grad_finish",
    )(x_in, cotangent, inv_rms, norm_gain[None], *values, *extra)


def over_columns(left, right):
    return lax.dot_general(left, right, (((1,), (1,)), ((), ())), preferred_element_type=f32)


def after(value, *others):
    return lax.optimization_barrier((value,) + others)[0]


def from_side(value):
    return lax.ppermute(value, "tensor", [(0, 1), (1, 0)])


def side_start(value):
    if lax.axis_size("tensor") == 2:
        return value, from_side(value)
    return None, lax.psum(value, "tensor")


def present(pair):
    return [value for value in pair if value is not None]


def side_total(pair):
    value, got = pair
    return got.astype(f32) if value is None else value.astype(f32) + got.astype(f32)


def pair_up(value, bit):
    size = lax.axis_size("dp")
    return lax.ppermute(value, "dp", [(i, i ^ bit) for i in range(size)])


def dealt_order(bits):
    order = [0]
    for bit in reversed(bits):
        order = order + [j | bit for j in order]
    return order


class Order:
    def __init__(self):
        self.pending = []

    def first(self, value):
        return after(value, *self.pending) if self.pending else value

    def then(self, value):
        self.pending = [value]
        return value

    def wait(self, value):
        self.pending = self.pending + [value]


def send_pieces(pieces, bit):
    return pieces[0], pair_up(pieces[1], bit)


def add_all(order, sent, kind=bf16):
    kept, got = sent
    return order.then(run_add([order.first(kept), got], 1, kind)[0])


def add_send(order, sent, bit):
    kept, got = sent
    pieces = run_add([order.first(kept), got], 2, bf16)
    order.then(pieces[0])
    return send_pieces(pieces, bit)


def add_last(order, sent, bits):
    for bit in bits:
        sent = add_send(order, sent, bit)
    return add_all(order, sent)


def send_same(value, bit):
    return value, pair_up(value, bit)


def local(
    x_in,
    norm_gain,
    w_zx,
    w_bc,
    w_dt,
    conv_x,
    conv_bc,
    dt_bias,
    a_log,
    d_skip,
    gate_gain,
    w_out,
    cotangent,
    block_parent,
):
    tokens, features = x_in.shape
    heads = w_dt.shape[1]
    inner = w_zx.shape[2]
    head_dim = inner // heads
    sides = lax.axis_size("tensor")
    dp = lax.axis_size("dp")
    full = inner * sides
    blocks = block_parent.shape[0]
    length = tokens // blocks
    wide = w_bc.shape[1]
    small = -(-(wide + heads) // 128) * 128
    window = conv_x.shape[0] - 1
    share = features // dp
    me = lax.axis_index("dp")

    near = []
    bit = 2
    while bit < dp:
        near.append(bit)
        bit *= 2
    far = near[1:] + near[:1]

    def places(bits):
        return lax.bitwise_xor(me, jnp.asarray(dealt_order(bits), jnp.int32)).astype(jnp.int32)

    place_near, place_far = places(near), places(far)

    head_of = jnp.arange(inner, dtype=jnp.int32) // head_dim
    one_hot = (jnp.arange(heads, dtype=jnp.int32)[:, None] == head_of[None, :]).astype(bf16)
    sel = jnp.concatenate([one_hot, one_hot], axis=0)
    sel_t = (jnp.arange(128, dtype=jnp.int32)[None, :] == head_of[:, None]).astype(bf16)
    skip_l = jnp.repeat(d_skip, head_dim)[None]

    count = blocks // 2
    step = count * length
    w_dt_t = w_dt.T
    join = lambda values: jnp.concatenate(values, axis=0)

    order = Order()
    normed, turned, inv_rms, bc_pre, dt_raw = run_norm(x_in, cotangent, norm_gain, w_bc, w_dt_t, length)
    turned_near = pair_up(turned, 1)
    w_cat = w_zx.reshape(features, 2 * inner)
    zx = jnp.dot(normed, w_cat, preferred_element_type=f32).astype(bf16)
    y, xc, pre, gg, bcc, bcp, hs, sq = run_forward(
        block_parent, bc_pre, dt_raw, zx, conv_x, conv_bc, dt_bias, a_log, skip_l, gate_gain, sel
    )
    gg_near = pair_up(gg, 1)
    out, cross = run_output(gg, w_out, cotangent)
    sums = side_total(side_start(join([sq[:, 0, :], cross[0].reshape(blocks, length)])))
    got_out = side_start(after(out, sums))
    dgn = over_columns(after(cotangent, out), w_out).astype(bf16)
    squares, crosses = sums[:blocks], sums[blocks:]
    inv_gate = lax.rsqrt(squares / full + epsilon)
    scale = inv_gate.reshape(1, tokens)
    scale = jnp.concatenate([scale, pair_up(scale, 1)], axis=1)
    dz, dy, gg_grad = run_ungate(squares, crosses, y, zx, dgn, gate_gain, full)
    order.then(dz)
    dz_near = pair_up(dz, 1)
    rights = [order.first(gg), gg_near]
    pieces = run_grad(place_near, 1, turned, turned_near, rights, share, 0, inner, 2, scale)
    order.then(pieces[0])
    w_out_1 = send_pieces(pieces, near[0])
    rights = [order.first(dz), dz_near]
    pieces = run_grad(place_near, 0, turned, turned_near, rights, share, 0, inner, 2)
    order.then(pieces[0])
    w_z_1 = send_pieces(pieces, near[0])

    tail = (conv_x, conv_bc, dt_bias, a_log, skip_l, sel, sel_t, small)
    back = run_backward(
        0, blocks, block_parent, order.first(dy), xc, pre, zx, hs, bcc, bcp, bc_pre, dt_raw, *tail, ()
    )
    dx, dbc, ddt, gkx, gkbc, gskip, ghead = back
    order.then(dx)
    order.wait(got_out[1])
    order.wait(w_out_1[1])
    w_out_2 = add_send(order, w_out_1, near[1])
    dx_near = pair_up(dx, 1)
    got_bc = side_start(dbc)
    low_1, gain_1 = run_input(dz, order.first(dx), dbc, ddt, w_cat, w_bc, w_dt_t, x_in, inv_rms, 0, step)
    order.then(low_1)
    got_low_1 = side_start(low_1)
    w_out_3 = add_send(order, w_out_2, near[2])
    got_bc = tuple(None if value is None else order.first(value) for value in got_bc)
    d_small = jnp.concatenate([side_total(got_bc).astype(bf16), ddt], axis=1)
    order.then(d_small)
    small_near = pair_up(d_small, 1)
    order.wait(dx_near)
    low_2, gain_2 = run_input(dz, order.first(dx), dbc, ddt, w_cat, w_bc, w_dt_t, x_in, inv_rms, 1, step)
    order.then(low_2)
    order.wait(small_near)
    got_low_2 = side_start(low_2)
    w_z_2 = add_send(order, w_z_1, near[1])
    edge = inner * 5 // 8 // 256 * 256
    pieces = run_grad(place_near, 0, turned, turned_near, [order.first(dx), dx_near], share, 0, edge, 2)
    order.then(pieces[1])
    sent_a = send_pieces(pieces, near[0])
    w_out_grad = add_last(order, w_out_3, near[3:])
    pieces = run_grad(place_near, 0, turned, turned_near, [order.first(d_small), small_near], share, 0, small, 2)
    order.then(pieces[1])
    sent_s = send_pieces(pieces, near[0])
    pieces = run_grad(place_far, 0, turned, turned_near, [order.first(dx), dx_near], share, edge, inner - edge, 2)
    order.then(pieces[1])
    w_z_3 = add_send(order, w_z_2, near[2])

    def finish(part, got, into):
        values = present(got)
        values = [order.first(values[0])] + values[1:]
        return order.then(
            run_finish(values, x_in, cotangent, inv_rms, norm_gain, part * count, length, into)
        )

    def spread_rows(sent, bit):
        kept, got = sent
        places_s.extend([j ^ bit for j in places_s])
        return order.then(join([order.first(kept), got]))

    places_s = [0]
    input_grad = finish(0, got_low_1, None)
    sent_b = send_pieces(pieces, far[0])
    sent_a = add_send(order, sent_a, near[1])
    sent_s = add_send(order, sent_s, near[1])
    mixed = order.then(run_mixed(squares, order.first(x_in), present(got_out), full))
    w_z_grad = add_last(order, w_z_3, near[3:])
    gain_1, gain_2, gkbc, gskip, gkx, ghead, gg_grad = order.first((gain_1, gain_2, gkbc, gskip, gkx, ghead, gg_grad))
    shared = jnp.concatenate([(gain_1 + gain_2).reshape(-1), gkbc.reshape(-1)])
    d_skip_part = jnp.sum(gskip.reshape(heads, head_dim), axis=1)
    own = jnp.concatenate(
        [gkx.reshape(-1), ghead.reshape(-1), d_skip_part, gg_grad.reshape(-1)]
    )
    n_shared, n_own = shared.shape[0], own.shape[0]
    pad_shared = -(-n_shared // 1024) * 1024
    pad_own = -(-n_own // 1024) * 1024
    shared = jnp.concatenate([shared, jnp.zeros((pad_shared - n_shared,), f32)]).reshape(-1, 128)
    own = jnp.concatenate([own, jnp.zeros((pad_own - n_own,), f32)]).reshape(-1, 128)
    packed = join([shared, own])

    order.then(packed)
    packed = send_same(packed, 1)
    sent_b = add_send(order, sent_b, far[1])
    packed = send_same(add_all(order, packed, f32), near[0])
    sent_a = add_send(order, sent_a, near[2])
    sent_s = add_send(order, sent_s, near[2])
    packed = send_same(add_all(order, packed, f32), near[1])
    order.wait(got_low_2[1])
    input_grad = finish(1, got_low_2, input_grad)
    w_s = add_last(order, sent_s, near[3:])
    rows_bc = send_same(w_s[:, :wide], near[2])
    sent_b = add_send(order, sent_b, far[2])
    packed = send_same(add_all(order, packed, f32), near[2])
    rows_bc = send_same(spread_rows(rows_bc, near[2]), near[1])
    w_x_a = add_last(order, sent_a, near[3:])
    packed = add_all(order, packed, f32)
    for bit in near[3:]:
        packed = add_all(order, send_same(packed, bit), f32)
    got_shared = side_start(packed[: pad_shared // 128])
    rows_bc = send_same(spread_rows(rows_bc, near[1]), near[0])
    w_x_b = add_last(order, sent_b, far[3:])
    rows_bc = spread_rows(rows_bc, near[0])
    for bit in near[3:]:
        rows_bc = spread_rows(send_same(rows_bc, bit), bit)
    rows_bc = spread_rows(send_same(rows_bc, 1), 1)
    chunks = rows_bc.reshape(dp, share, wide)
    back_to = jnp.asarray([places_s.index(j) for j in range(dp)], jnp.int32)
    w_bc_grad = jnp.take(chunks, back_to[lax.bitwise_xor(me, jnp.arange(dp, dtype=jnp.int32))], axis=0)
    w_bc_grad = w_bc_grad.reshape(features, wide).astype(f32)
    w_dt_grad = w_s[:, wide : wide + heads].astype(f32)
    w_x_grad = jnp.concatenate([w_x_a, w_x_b], axis=1)
    shared = side_total(got_shared).reshape(-1)
    own = packed[pad_shared // 128 :].reshape(-1)

    edge = (window + 1) * inner
    w_zx_grad = jnp.stack([w_z_grad, w_x_grad], axis=1).astype(f32)
    return (
        mixed,
        input_grad,
        shared[:features],
        w_zx_grad,
        w_bc_grad,
        w_dt_grad,
        own[:edge].reshape(window + 1, inner),
        shared[features:n_shared].reshape(window + 1, wide),
        own[edge : edge + heads],
        own[edge + heads : edge + 2 * heads],
        own[edge + 2 * heads : edge + 3 * heads],
        own[edge + 3 * heads : n_own],
        w_out_grad.astype(f32).T,
    )


def solution(mesh):
    return jax.shard_map(
        local,
        mesh=mesh,
        in_specs=(
            P("dp", None),
            P(),
            P(None, None, "tensor"),
            P(),
            P(None, "tensor"),
            P(None, "tensor"),
            P(),
            P("tensor"),
            P("tensor"),
            P("tensor"),
            P("tensor"),
            P("tensor", None),
            P("dp", None),
            P("dp"),
        ),
        out_specs=(
            P("dp", None),
            P("dp", None),
            P(),
            P("dp", None, "tensor"),
            P(),
            P("dp", "tensor"),
            P(None, "tensor"),
            P(),
            P("tensor"),
            P("tensor"),
            P("tensor"),
            P("tensor"),
            P("tensor", "dp"),
        ),
        check_vma=False,
    )
```

```python
import functools

import jax
import jax.numpy as jnp
from jax import lax
from jax.experimental import pallas as pl
from jax.experimental.pallas import tpu as pltpu
from jax.sharding import PartitionSpec as P

epsilon = 1e-05
f32 = jnp.float32
bf16 = jnp.bfloat16
VMEM_LIMIT = 60 * 1024 * 1024
LIGHT = pl.CostEstimate(flops=1000, bytes_accessed=1000, transcendentals=0)


def sigmoid(v):
    return 0.5 * jnp.tanh(0.5 * v) + 0.5


def dot(a, b, dims=((1,), (0,)), precision=None):
    return lax.dot_general(a, b, (dims, ((), ())), precision=precision, preferred_element_type=f32)


NN = ((1,), (0,))
NT = ((1,), (1,))
TN = ((0,), (0,))
highest = lax.Precision.HIGHEST


def split_low(v):
    hi = v.astype(bf16)
    lo = (v - hi.astype(f32)).astype(bf16)
    return hi, lo


def head_masks(length, head_dim):
    lane = lax.broadcasted_iota(jnp.int32, (length, 2 * head_dim), 1)
    return lane < head_dim


def pair_stack(v, first):
    zero = jnp.zeros_like(v)
    return jnp.concatenate([jnp.where(first, v, zero), jnp.where(first, zero, v)], axis=0)


def tri_mask(length):
    row = lax.broadcasted_iota(jnp.int32, (length, length), 0)
    col = lax.broadcasted_iota(jnp.int32, (length, length), 1)
    return row, col


def step_values(dtr_ref, bias_ref, alog_ref, length):
    row, col = tri_mask(length)
    dtr = dtr_ref[...] + bias_ref[...]
    dt = jnp.maximum(dtr, 0.0) + jnp.log1p(jnp.exp(-jnp.abs(dtr)))
    rate = -jnp.exp(alog_ref[...])
    tri = (row >= col).astype(f32)
    cum = dot(tri, dt * rate, NN, highest)
    last = cum[length - 1 : length, :]
    return dtr, dt, rate, cum, jnp.exp(cum), jnp.exp(jnp.minimum(last - cum, 0.0))


def store_columns(cum, cum_s, cumt_s, heads):
    cum_s[:, :heads] = cum
    cumt_s[...] = jnp.transpose(cum_s[...])


def conv_rows(ext, kern, length, window):
    base = ext.shape[0] - length - (window - 1)
    total = kern[window : window + 1, :] + kern[window - 1 : window, :] * ext[ext.shape[0] - length :, :]
    for offset in range(window - 1):
        total = total + kern[offset : offset + 1, :] * ext[base + offset : base + offset + length, :]
    return total


def forward_kernel(
    sizes,
    par_ref,
    bc_ref,
    dtr_ref,
    z_ref,
    xp_ref,
    dgn_ref,
    kx_ref,
    kbc_ref,
    bias_ref,
    alog_ref,
    skip_ref,
    gain_ref,
    sel_ref,
    y_ref,
    xc_ref,
    pre_ref,
    gg_ref,
    bcc_ref,
    bcp_ref,
    hs_ref,
    sq_ref,
    h_end,
    tail_x,
    tail_bc,
    lhs_s,
    cum_s,
    cumt_s,
    score_s,
    acc_s,
    cross_s,
):
    length, inner, heads, head_dim, lanes, blocks, window = sizes
    state = bcc_ref.shape[1] // 2
    b = pl.program_id(0)
    par = par_ref[b]
    slot = jnp.where(par >= 0, par, blocks)

    @pl.when(b == 0)
    def _():
        h_end[blocks] = jnp.zeros(h_end.shape[1:], f32)
        tail_x[blocks] = jnp.zeros(tail_x.shape[1:], f32)
        tail_bc[blocks] = jnp.zeros(tail_bc.shape[1:], f32)
        cum_s[...] = jnp.zeros_like(cum_s)

    bcv = bc_ref[...]
    pre = conv_rows(jnp.concatenate([tail_bc[slot], bcv], axis=0), kbc_ref[...], length, window)
    tail_bc[b] = bcv[length - 8 :, :]
    bcc = (pre * sigmoid(pre)).astype(bf16)
    bcc_ref[...] = bcc
    bcp_ref[...] = pre
    c_rows = bcc[:, state:]
    b_rows = bcc[:, :state]
    row, col = tri_mask(length)
    score_s[...] = jnp.where(row >= col, dot(c_rows, b_rows, NT), 0.0)

    _, dt, _, cum, from_start, to_end = step_values(dtr_ref, bias_ref, alog_ref, length)
    hi, lo = split_low(jnp.concatenate([dt, from_start, to_end], axis=0))
    lhs_s[...] = jnp.concatenate([hi, lo], axis=1)
    store_columns(cum, cum_s, cumt_s, heads)
    acc_s[...] = jnp.zeros_like(acc_s)
    cross_s[...] = jnp.zeros_like(cross_s)
    first = head_masks(length, head_dim)
    group = lanes // head_dim
    pair = 2 * head_dim

    def body(g, carry):
        sl = pl.ds(pl.multiple_of(g * lanes, lanes), lanes)
        xpv = xp_ref[:, sl].astype(f32)
        ext = jnp.concatenate([tail_x[slot, :, sl], xpv], axis=0)
        pre_x = conv_rows(ext, kx_ref[:, sl], length, window)
        tail_x[b, :, sl] = xpv[length - 8 :, :]
        xc = (pre_x * sigmoid(pre_x)).astype(bf16)
        pre_ref[:, sl] = pre_x.astype(bf16)
        xc_ref[:, sl] = xc
        wide = dot(lhs_s[...], sel_ref[:, sl])
        dt_l = wide[:length]
        start_l = wide[length : 2 * length]
        end_l = wide[2 * length :]
        xcf = xc.astype(f32)
        xd = dt_l * xcf
        xdb = xd.astype(bf16)
        gx = (end_l * xd).astype(bf16)
        h = h_end[slot, :, sl]
        hb = h.astype(bf16)
        hs_ref[0, :, sl] = hb
        carried = start_l * dot(c_rows, hb)
        h_end[b, :, sl] = start_l[length - 1 : length, :] * h + dot(b_rows, gx, TN)
        cols = pltpu.roll(cum_s[...], cum_s.shape[1] - g * group, 1)
        rows = cumt_s[pl.ds(pl.multiple_of(g * group, 8), max(group, 8)), :]
        score = score_s[...]
        skip = skip_ref[:, sl]
        gain = gain_ref[:, sl]
        zv = z_ref[:, sl].astype(f32)
        gate = zv * sigmoid(zv)
        acc = acc_s[...]
        cross = cross_s[...]
        dgn = dgn_ref[:, sl].astype(f32)
        for q in range(lanes // pair):
            at = slice(q * pair, (q + 1) * pair)
            weights = []
            for h_at in (2 * q, 2 * q + 1):
                gap = jnp.minimum(cols[:, h_at : h_at + 1] - rows[h_at : h_at + 1, :], 0.0)
                weights.append((score * jnp.exp(gap)).astype(bf16))
            within = dot(jnp.concatenate(weights, axis=1), pair_stack(xdb[:, at], first))
            y = (within + carried[:, at] + skip[:, at] * xcf[:, at]).astype(bf16)
            out = pl.ds(pl.multiple_of(g * lanes + q * pair, pair), pair)
            y_ref[:, out] = y
            gated = y.astype(f32) * gate[:, at]
            gained = gated * gain[:, at]
            gg_ref[:, out] = gained.astype(bf16)
            acc = acc + gated * gated
            cross = cross + dgn[:, at] * gained
        acc_s[...] = acc
        cross_s[...] = cross
        return carry

    lax.fori_loop(0, inner // lanes, body, 0)
    ones = jnp.ones((8, pair), f32)
    sq_ref[0, :8, :] = dot(ones, acc_s[...], NT, highest)
    sq_ref[0, 8:, :] = dot(ones, cross_s[...], NT, highest)


def run_forward(parent, bc_pre, dt_raw, zx, dgn, conv_x, conv_bc, dt_bias, a_log, skip_l, gate_gain, sel):
    tokens = zx.shape[0]
    inner = conv_x.shape[1]
    heads = dt_raw.shape[1]
    head_dim = inner // heads
    blocks = parent.shape[0]
    length = tokens // blocks
    window = conv_x.shape[0] - 1
    wide = bc_pre.shape[1]
    state = wide // 2
    lanes = min(512, inner)
    sizes = (length, inner, heads, head_dim, lanes, blocks, window)
    whole = lambda shape: pl.BlockSpec(shape, lambda b, *_: (0,) * len(shape))
    rows = lambda width: pl.BlockSpec((length, width), lambda b, *_: (b, 0))
    block = lambda shape: pl.BlockSpec((1,) + shape, lambda b, *_: (b, 0, 0))
    grid_spec = pltpu.PrefetchScalarGridSpec(
        num_scalar_prefetch=1,
        grid=(blocks,),
        in_specs=[
            rows(wide),
            rows(heads),
            rows(inner),
            pl.BlockSpec((length, inner), lambda b, *_: (b, 1)),
            rows(inner),
            whole(conv_x.shape),
            whole(conv_bc.shape),
            whole((1, heads)),
            whole((1, heads)),
            whole((1, inner)),
            whole((1, inner)),
            whole(sel.shape),
        ],
        out_specs=[
            rows(inner),
            rows(inner),
            rows(inner),
            rows(inner),
            rows(wide),
            rows(wide),
            block((state, inner)),
            block((16, length)),
        ],
        scratch_shapes=[
            pltpu.VMEM((blocks + 1, state, inner), f32),
            pltpu.VMEM((blocks + 1, 8, inner), f32),
            pltpu.VMEM((blocks + 1, 8, wide), f32),
            pltpu.VMEM((3 * length, 2 * heads), bf16),
            pltpu.VMEM((length, length), f32),
            pltpu.VMEM((length, length), f32),
            pltpu.VMEM((length, length), f32),
            pltpu.VMEM((length, 2 * head_dim), f32),
            pltpu.VMEM((length, 2 * head_dim), f32),
        ],
    )
    return pl.pallas_call(
        functools.partial(forward_kernel, sizes),
        grid_spec=grid_spec,
        out_shape=[jax.ShapeDtypeStruct((tokens, inner), bf16)] * 4
        + [
            jax.ShapeDtypeStruct((tokens, wide), bf16),
            jax.ShapeDtypeStruct((tokens, wide), f32),
            jax.ShapeDtypeStruct((blocks, state, inner), bf16),
            jax.ShapeDtypeStruct((blocks, 16, length), f32),
        ],
        compiler_params=pltpu.CompilerParams(vmem_limit_bytes=VMEM_LIMIT),
        cost_estimate=LIGHT,
        name="ssd_forward",
    )(parent, bc_pre, dt_raw, zx, zx, dgn, conv_x, conv_bc, dt_bias[None], a_log[None], skip_l, gate_gain[None], sel)


def token_column(row_ref, at, length):
    row = row_ref[pl.ds(at, 1), :]
    return jnp.transpose(jnp.broadcast_to(row, (length, length)))


def ungate_kernel(sizes, sq_ref, cross_ref, y_ref, z_ref, dgn_ref, gain_ref, dz_ref, dy_ref, grad_ref):
    length, inner, lanes, full = sizes
    b = pl.program_id(0)
    inv = lax.rsqrt(token_column(sq_ref, b, length) / full + epsilon)
    coef = inv * token_column(cross_ref, b, length) / full

    @pl.when(b == 0)
    def _():
        grad_ref[...] = jnp.zeros_like(grad_ref)

    def body(g, carry):
        sl = pl.ds(pl.multiple_of(g * length, length), length)
        zv = z_ref[:, sl].astype(f32)
        sig = sigmoid(zv)
        gate = zv * sig
        gain = gain_ref[:, sl]
        y = y_ref[:, sl].astype(f32) * inv
        scaled = y * gate
        dgn = dgn_ref[:, sl].astype(f32)
        grad_ref[:, sl] += jnp.sum(dgn * scaled, axis=0, keepdims=True)
        d_scaled = dgn * gain - scaled * coef
        dz_ref[:, sl] = (d_scaled * y * (sig + gate * (1.0 - sig))).astype(bf16)
        dy_ref[:, sl] = (d_scaled * inv * gate).astype(bf16)
        return carry

    lax.fori_loop(0, inner // length, body, 0, unroll=2)


def run_ungate(squares, cross, y, zx, dgn, gate_gain, full):
    tokens, inner = y.shape
    blocks, length = squares.shape
    rows = pl.BlockSpec((length, inner), lambda b: (b, 0))
    one = pl.BlockSpec((1, inner), lambda b: (0, 0))
    small = pl.BlockSpec((blocks, length), lambda b: (0, 0))
    return pl.pallas_call(
        functools.partial(ungate_kernel, (length, inner, length, full)),
        grid=(blocks,),
        in_specs=[small, small, rows, rows, rows, one],
        out_specs=[rows, rows, one],
        out_shape=[jax.ShapeDtypeStruct((tokens, inner), bf16)] * 2 + [jax.ShapeDtypeStruct((1, inner), f32)],
        compiler_params=pltpu.CompilerParams(vmem_limit_bytes=VMEM_LIMIT),
        cost_estimate=LIGHT,
        name="gate_backward",
    )(squares, cross, y, zx, dgn, gate_gain[None])


def norm_kernel(features, x_ref, cot_ref, gain_ref, wbc_ref, wdt_ref, normed_ref, turned_ref, inv_ref, bc_ref, dtr_ref):
    x = x_ref[...].astype(f32)
    inv = lax.rsqrt(jnp.sum(x * x, axis=1, keepdims=True) / features + epsilon)
    inv_ref[...] = inv
    normed = (x * inv * gain_ref[...]).astype(bf16)
    normed_ref[...] = normed
    turned_ref[0] = jnp.transpose(normed)
    turned_ref[1] = jnp.transpose(cot_ref[...])
    bc_ref[...] = dot(normed, wbc_ref[...])
    dtr_ref[...] = dot(normed, wdt_ref[...], NT)


def run_norm(x_in, cotangent, norm_gain, w_bc, w_dt_t, length):
    tokens, features = x_in.shape
    wide = w_bc.shape[1]
    heads = w_dt_t.shape[0]
    rows = lambda width: pl.BlockSpec((length, width), lambda b: (b, 0))
    whole = lambda shape: pl.BlockSpec(shape, lambda b: (0, 0), pipeline_mode=pl.Buffered(1))
    turned = pl.BlockSpec((2, features, length), lambda b: (0, 0, b))
    return pl.pallas_call(
        functools.partial(norm_kernel, features),
        grid=(tokens // length,),
        in_specs=[rows(features), rows(features), whole((1, features)), whole(w_bc.shape), whole(w_dt_t.shape)],
        out_specs=[rows(features), turned, rows(1), rows(wide), rows(heads)],
        out_shape=[
            jax.ShapeDtypeStruct((tokens, features), bf16),
            jax.ShapeDtypeStruct((2, features, tokens), bf16),
            jax.ShapeDtypeStruct((tokens, 1), f32),
            jax.ShapeDtypeStruct((tokens, wide), f32),
            jax.ShapeDtypeStruct((tokens, heads), f32),
        ],
        compiler_params=pltpu.CompilerParams(vmem_limit_bytes=VMEM_LIMIT),
        cost_estimate=LIGHT,
        name="input_norm",
    )(x_in, cotangent, norm_gain[None], w_bc, w_dt_t)


def fetch_left(share, which, place_ref, mine_ref, theirs_ref, left_s, sem):
    tokens = mine_ref.shape[2]
    count = left_s.shape[0] // share
    copies = []
    for i in range(count):
        src = pl.ds(pl.multiple_of(place_ref[i] * share, share), share)
        for side, ref in enumerate((mine_ref, theirs_ref)):
            copies.append(
                pltpu.make_async_copy(
                    ref.at[which, src, :],
                    left_s.at[pl.ds(i * share, share), pl.ds(side * tokens, tokens)],
                    sem.at[2 * i + side],
                )
            )
    return copies


def gather_right(refs, right_s):
    at = 0
    for ref in refs:
        size = ref.shape[0]
        right_s[at : at + size, :] = ref[...]
        at += size


def load_left(share, which, place_ref, mine_ref, theirs_ref, left_s, sem):
    copies = fetch_left(share, which, place_ref, mine_ref, theirs_ref, left_s, sem)
    for copy in copies:
        copy.start()
    for copy in copies:
        copy.wait()


def grad_kernel(share, which, pieces, scaled, outs, place_ref, mine_ref, theirs_ref, *rest):
    rights = rest[:pieces]
    rest = rest[pieces:]
    if scaled:
        scale_ref = rest[0]
        rest = rest[1:]
    out_refs = rest[:outs]
    left_s, right_s, sem = rest[outs:]

    @pl.when(pl.program_id(0) == 0)
    def _():
        load_left(share, which, place_ref, mine_ref, theirs_ref, left_s, sem)
        if scaled:
            rows_at = left_s.shape[0] // 8

            def apply(i, carry):
                at = pl.ds(pl.multiple_of(i * rows_at, rows_at), rows_at)
                left_s[at, :] = (left_s[at, :].astype(f32) * scale_ref[...]).astype(bf16)
                return carry

            lax.fori_loop(0, 8, apply, 0)

    gather_right(rights, right_s)
    total = dot(left_s[...], right_s[...])
    size = out_refs[0].shape[0]
    for i, ref in enumerate(out_refs):
        ref[...] = total[i * size : (i + 1) * size].astype(bf16)


def run_grad(places, which, mine, theirs, rights, share, first, width, outs, scale=None):
    tokens = mine.shape[2]
    count = places.shape[0]
    rows = count * share
    tile = 256 if width % 256 == 0 and first % 256 == 0 else 128
    anywhere = pl.BlockSpec(memory_space=pl.ANY)
    columns = [
        pl.BlockSpec((right.shape[0], tile), lambda j, *_: (0, first // tile + j)) for right in rights
    ]
    extra = [] if scale is None else [pl.BlockSpec(scale.shape, lambda j, *_: (0, 0))]
    return pl.pallas_call(
        functools.partial(grad_kernel, share, which, len(rights), scale is not None, outs),
        grid_spec=pltpu.PrefetchScalarGridSpec(
            num_scalar_prefetch=1,
            grid=(width // tile,),
            in_specs=[anywhere, anywhere] + columns + extra,
            out_specs=[pl.BlockSpec((rows // outs, tile), lambda j, *_: (0, j))] * outs,
            scratch_shapes=[
                pltpu.VMEM((rows, 2 * tokens), bf16),
                pltpu.VMEM((2 * tokens, tile), bf16),
                pltpu.SemaphoreType.DMA((2 * count,)),
            ],
        ),
        out_shape=[jax.ShapeDtypeStruct((rows // outs, width), bf16)] * outs,
        compiler_params=pltpu.CompilerParams(vmem_limit_bytes=VMEM_LIMIT),
        cost_estimate=LIGHT,
        name="weight_grad",
    )(places, mine, theirs, *rights, *([] if scale is None else [scale]))


def input_kernel(heads, dz_ref, dx_ref, dbc_ref, ddt_ref, wz_ref, wx_ref, wbc_ref, wdt_ref, x_ref, inv_ref, out_ref, gain_ref):
    total = dot(dz_ref[...], wz_ref[...], NT) + dot(dx_ref[...], wx_ref[...], NT)
    total = total + dot(dbc_ref[...], wbc_ref[...], NT)
    total = total + dot(ddt_ref[:, :heads], wdt_ref[...], NN)
    out_ref[...] = total.astype(bf16)
    gain_ref[...] = jnp.sum(total * (x_ref[...].astype(f32) * inv_ref[...]), axis=0, keepdims=True)


def run_input(dz, dx, dbc, ddt, w_cat, w_bc, w_dt_t, x_in, inv_rms, at, tokens):
    inner = dz.shape[1]
    features = x_in.shape[1]
    wide = w_bc.shape[1]
    heads = w_dt_t.shape[0]
    tile = 256
    side = lambda width: pl.BlockSpec((tokens, width), lambda j: (at, 0), pipeline_mode=pl.Buffered(1))
    return pl.pallas_call(
        functools.partial(input_kernel, heads),
        grid=(features // tile,),
        in_specs=[
            side(inner),
            side(inner),
            side(wide),
            side(ddt.shape[1]),
            pl.BlockSpec((tile, inner), lambda j: (j, 0)),
            pl.BlockSpec((tile, inner), lambda j: (j, 1)),
            pl.BlockSpec((tile, wide), lambda j: (j, 0)),
            pl.BlockSpec((heads, tile), lambda j: (0, j)),
            pl.BlockSpec((tokens, tile), lambda j: (at, j)),
            pl.BlockSpec((tokens, 1), lambda j: (at, 0)),
        ],
        out_specs=[pl.BlockSpec((tokens, tile), lambda j: (0, j)), pl.BlockSpec((1, tile), lambda j: (0, j))],
        out_shape=[jax.ShapeDtypeStruct((tokens, features), bf16), jax.ShapeDtypeStruct((1, features), f32)],
        compiler_params=pltpu.CompilerParams(vmem_limit_bytes=VMEM_LIMIT),
        cost_estimate=pl.CostEstimate(flops=27 * 900_000_000, bytes_accessed=1000, transcendentals=0),
        name="input_grad",
    )(dz, dx, dbc, ddt, w_cat, w_cat, w_bc, w_dt_t, x_in, inv_rms)


def conv_back(ext, kern, inputs, length, window):
    total = kern[window - 1 : window, :] * ext[:length, :]
    sums = [None] * (window + 1)
    sums[window] = jnp.sum(ext[:length, :], axis=0, keepdims=True)
    sums[window - 1] = jnp.sum(inputs * ext[:length, :], axis=0, keepdims=True)
    for shift in range(1, window):
        moved = ext[shift : shift + length, :]
        total = total + kern[window - 1 - shift : window - shift, :] * moved
        sums[window - 1 - shift] = jnp.sum(inputs * moved, axis=0, keepdims=True)
    return total, jnp.concatenate(sums, axis=0)


def backward_kernel(
    sizes,
    par_ref,
    dy_ref,
    xc_ref,
    pre_ref,
    xp_ref,
    hs_ref,
    bcc_ref,
    bcp_ref,
    bc_ref,
    dtr_ref,
    kx_ref,
    kbc_ref,
    bias_ref,
    alog_ref,
    skip_ref,
    sel_ref,
    selt_ref,
    *rest,
):
    length, inner, heads, head_dim, lanes, blocks, window, start, count = sizes
    last_chunk = start + count == blocks
    if not last_chunk:
        ds_prev, nx_prev, nbc_prev = rest[:3]
        rest = rest[3:]
    dxp_ref, dbc_ref, ddt_ref, gkx_ref, gkbc_ref, gskip_ref, ghead_ref = rest[:7]
    rest = rest[7:]
    if start:
        ds_next, nx_next, nbc_next = rest[:3]
        rest = rest[3:]
    (
        d_state,
        next_x,
        next_bc,
        lhs_s,
        cum_s,
        cumt_s,
        score_s,
        dscore_s,
        db_s,
        dc_s,
        red_s,
        cross_s,
        inner_s,
    ) = rest
    state = bcc_ref.shape[1] // 2
    b = start + count - 1 - pl.program_id(0)
    par = par_ref[b]
    slot = jnp.where(par >= 0, par, blocks)

    @pl.when(pl.program_id(0) == 0)
    def _():
        if last_chunk:
            d_state[...] = jnp.zeros_like(d_state)
            next_x[...] = jnp.zeros_like(next_x)
            next_bc[...] = jnp.zeros_like(next_bc)
        else:
            pltpu.sync_copy(ds_prev, d_state.at[: start + count])
            next_x[: start + count] = nx_prev[...]
            next_bc[: start + count] = nbc_prev[...]
            d_state[blocks] = jnp.zeros(d_state.shape[1:], f32)
            next_x[blocks] = jnp.zeros(next_x.shape[1:], f32)
            next_bc[blocks] = jnp.zeros(next_bc.shape[1:], f32)
        cum_s[...] = jnp.zeros_like(cum_s)
        cross_s[...] = jnp.zeros_like(cross_s)
        gkx_ref[...] = jnp.zeros_like(gkx_ref)
        gkbc_ref[...] = jnp.zeros_like(gkbc_ref)
        gskip_ref[...] = jnp.zeros_like(gskip_ref)
        ghead_ref[...] = jnp.zeros_like(ghead_ref)

    bcc = bcc_ref[...]
    c_rows = bcc[:, state:]
    b_rows = bcc[:, :state]
    row, col = tri_mask(length)
    score_s[...] = jnp.where(row >= col, dot(c_rows, b_rows, NT), 0.0)
    dtr, dt, rate, cum, from_start, to_end = step_values(dtr_ref, bias_ref, alog_ref, length)
    hi, lo = split_low(jnp.concatenate([dt, from_start, to_end], axis=0))
    lhs_s[...] = jnp.concatenate([hi, lo], axis=1)
    store_columns(cum, cum_s, cumt_s, heads)
    dscore_s[...] = jnp.zeros_like(dscore_s)
    db_s[...] = jnp.zeros_like(db_s)
    dc_s[...] = jnp.zeros_like(dc_s)
    red_s[...] = jnp.zeros_like(red_s)
    first = head_masks(length, head_dim)
    group = lanes // head_dim
    pair = 2 * head_dim
    before = (row < col).astype(bf16)
    following = (row >= col).astype(f32)

    def body(g, carry):
        sl = pl.ds(pl.multiple_of(g * lanes, lanes), lanes)
        wide = dot(lhs_s[...], sel_ref[:, sl])
        dt_l = wide[:length]
        start_l = wide[length : 2 * length]
        end_l = wide[2 * length :]
        last_l = start_l[length - 1 : length, :]
        dyb = dy_ref[:, sl]
        dy = dyb.astype(f32)
        xc = xc_ref[:, sl]
        xcf = xc.astype(f32)
        xd = dt_l * xcf
        xdb = xd.astype(bf16)
        gx = (end_l * xd).astype(bf16)
        hb = hs_ref[0, :, sl]
        d_end = d_state[b, :, sl]
        d_endb = d_end.astype(bf16)
        sdy = (start_l * dy).astype(bf16)
        carried = start_l * dot(c_rows, hb)
        local = end_l * dot(b_rows, d_endb)
        dc_s[...] += dot(sdy, hb, NT)
        db_s[...] += dot(gx, d_endb, NT)
        d_state[slot, :, sl] += last_l * d_end + dot(c_rows, sdy, TN)
        carry_end = jnp.sum(d_end * hb.astype(f32), axis=0, keepdims=True) * last_l
        cols = pltpu.roll(cum_s[...], cum_s.shape[1] - g * group, 1)
        rows = cumt_s[pl.ds(pl.multiple_of(g * group, 8), max(group, 8)), :]
        score = score_s[...]
        dscore = dscore_s[...]
        crossings = []
        for q in range(lanes // pair):
            at = slice(q * pair, (q + 1) * pair)
            dy2 = pair_stack(dyb[:, at], first)
            dw2 = dot(dy2, xdb[:, at], NT)
            weights, terms = [], []
            for half in range(2):
                h_at = 2 * q + half
                gap = jnp.minimum(cols[:, h_at : h_at + 1] - rows[h_at : h_at + 1, :], 0.0)
                decay = jnp.exp(gap)
                weights.append((score * decay).astype(bf16))
                t = dw2[half * length : (half + 1) * length] * decay
                dscore = dscore + t
                terms.append((t * score).astype(bf16))
            inner_s[:, at] = dot(jnp.concatenate(weights, axis=0), dy2, TN)
            crossed = dot(jnp.concatenate(terms, axis=0), before)
            for half in range(2):
                part = crossed[half * length : (half + 1) * length] * following
                crossings.append(jnp.sum(part, axis=0, keepdims=True))
        dscore_s[...] = dscore
        cross_s[pl.ds(pl.multiple_of(g * group, 8), group), :] = jnp.concatenate(crossings, axis=0)
        dxd = inner_s[...] + local
        products = jnp.concatenate(
            [(dy * carried).astype(bf16), (local * xd).astype(bf16), (dxd * xcf).astype(bf16),
             jnp.broadcast_to(carry_end, (16, lanes)).astype(bf16)], axis=0
        )
        red_s[...] += dot(products, selt_ref[sl, :])
        gskip_ref[:, sl] += jnp.sum(dy * xcf, axis=0, keepdims=True)
        dx = dt_l * dxd + skip_ref[:, sl] * dy
        pre = pre_ref[:, sl].astype(f32)
        sig = sigmoid(pre)
        d_pre = dx * (sig + pre * sig * (1.0 - sig))
        ext = jnp.concatenate([d_pre, next_x[b, :, sl]], axis=0)
        next_x[slot, :, sl] += d_pre[:8, :]
        xpv = xp_ref[:, sl].astype(f32)
        dxp, sums = conv_back(ext, kx_ref[:, sl], xpv, length, window)
        dxp_ref[:, sl] = dxp.astype(bf16)
        gkx_ref[:, sl] += sums
        return carry

    lax.fori_loop(0, inner // lanes, body, 0)

    red = red_s[...]
    carried_t = red[:length, :heads]
    local_t = red[length : 2 * length, :heads]
    ddt = red[2 * length : 3 * length, :heads]
    end_t = red[3 * length : 3 * length + 1, :heads]
    suffix = (row <= col).astype(f32)
    prefix = (row > col).astype(f32)
    d_rate = (
        dot(suffix, carried_t, NN, highest)
        + dot(prefix, local_t, NN, highest)
        + end_t
        + jnp.transpose(cross_s[...])[:, :heads]
    )
    ddt = ddt + d_rate * rate
    ddtr = ddt * sigmoid(dtr)
    ghead_ref[0:1, :] += jnp.sum(ddtr, axis=0, keepdims=True)
    ghead_ref[1:2, :] += jnp.sum(d_rate * rate * dt, axis=0, keepdims=True)

    dscore = jnp.where(row >= col, dscore_s[...], 0.0).astype(bf16)
    d_c = dc_s[...] + dot(dscore, b_rows)
    d_b = db_s[...] + dot(dscore, c_rows, TN)
    pre = bcp_ref[...]
    sig = sigmoid(pre)
    d_pre = jnp.concatenate([d_b, d_c], axis=1) * (sig + pre * sig * (1.0 - sig))
    ext = jnp.concatenate([d_pre, next_bc[b]], axis=0)
    next_bc[slot] += d_pre[:8, :]
    dbcp, sums = conv_back(ext, kbc_ref[...], bc_ref[...], length, window)
    gkbc_ref[...] += sums
    dbc_ref[...] = dbcp.astype(bf16)
    ddt_ref[...] = jnp.zeros_like(ddt_ref)
    ddt_ref[:, :heads] = ddtr.astype(bf16)

    if start:

        @pl.when(b == start)
        def _():
            pltpu.sync_copy(d_state.at[:start], ds_next)
            nx_next[...] = next_x[:start]
            nbc_next[...] = next_bc[:start]


def run_backward(
    start, count, parent, dy, xc, pre, zx, hs, bcc, bcp, bc_pre, dt_raw, conv_x, conv_bc, dt_bias, a_log, skip_l,
    sel, sel_t, small, carry
):
    inner = conv_x.shape[1]
    heads = dt_raw.shape[1]
    head_dim = inner // heads
    blocks = parent.shape[0]
    length = dy.shape[0] // blocks
    tokens = count * length
    window = conv_x.shape[0] - 1
    wide = bcc.shape[1]
    state = wide // 2
    lanes = min(512, inner)
    anywhere = pl.BlockSpec(memory_space=pl.ANY)
    sizes = (length, inner, heads, head_dim, lanes, blocks, window, start, count)
    top = count - 1
    later = lambda width: pl.BlockSpec((length, width), lambda b, *_: (start + top - b, 0))
    whole = lambda shape: pl.BlockSpec(shape, lambda b, *_: (0,) * len(shape))
    rows = lambda width: pl.BlockSpec((length, width), lambda b, *_: (top - b, 0))
    carry_specs = [anywhere, whole(carry[1].shape), whole(carry[2].shape)] if carry else []
    next_specs, next_shapes = [], []
    if start:
        shapes = [(start, state, inner), (start, 8, inner), (start, 8, wide)]
        next_specs = [anywhere, whole(shapes[1]), whole(shapes[2])]
        next_shapes = [jax.ShapeDtypeStruct(shape, f32) for shape in shapes]
    grid_spec = pltpu.PrefetchScalarGridSpec(
        num_scalar_prefetch=1,
        grid=(count,),
        in_specs=[
            later(inner),
            later(inner),
            later(inner),
            pl.BlockSpec((length, inner), lambda b, *_: (start + top - b, 1)),
            pl.BlockSpec((1, state, inner), lambda b, *_: (start + top - b, 0, 0)),
            later(wide),
            later(wide),
            later(wide),
            later(heads),
            whole(conv_x.shape),
            whole(conv_bc.shape),
            whole((1, heads)),
            whole((1, heads)),
            whole((1, inner)),
            whole(sel.shape),
            whole(sel_t.shape),
        ]
        + carry_specs,
        out_specs=[
            rows(inner),
            rows(wide),
            rows(small - wide),
            whole(conv_x.shape),
            whole(conv_bc.shape),
            whole((1, inner)),
            whole((2, heads)),
        ]
        + next_specs,
        scratch_shapes=[
            pltpu.VMEM((blocks + 1, state, inner), f32),
            pltpu.VMEM((blocks + 1, 8, inner), f32),
            pltpu.VMEM((blocks + 1, 8, wide), f32),
            pltpu.VMEM((3 * length, 2 * heads), bf16),
            pltpu.VMEM((length, length), f32),
            pltpu.VMEM((length, length), f32),
            pltpu.VMEM((length, length), f32),
            pltpu.VMEM((length, length), f32),
            pltpu.VMEM((length, state), f32),
            pltpu.VMEM((length, state), f32),
            pltpu.VMEM((3 * length + 16, sel_t.shape[1]), f32),
            pltpu.VMEM((length, length), f32),
            pltpu.VMEM((length, lanes), f32),
        ],
    )
    return pl.pallas_call(
        functools.partial(backward_kernel, sizes),
        grid_spec=grid_spec,
        out_shape=[
            jax.ShapeDtypeStruct((tokens, inner), bf16),
            jax.ShapeDtypeStruct((tokens, wide), bf16),
            jax.ShapeDtypeStruct((tokens, small - wide), bf16),
            jax.ShapeDtypeStruct(conv_x.shape, f32),
            jax.ShapeDtypeStruct(conv_bc.shape, f32),
            jax.ShapeDtypeStruct((1, inner), f32),
            jax.ShapeDtypeStruct((2, heads), f32),
        ]
        + next_shapes,
        compiler_params=pltpu.CompilerParams(vmem_limit_bytes=VMEM_LIMIT),
        cost_estimate=LIGHT,
        name="ssd_backward",
    )(
        parent, dy, xc, pre, zx, hs, bcc, bcp, bc_pre, dt_raw, conv_x, conv_bc,
        dt_bias[None], a_log[None], skip_l, sel, sel_t, *carry,
    )


def add_kernel(terms, *refs):
    out_refs = refs[terms:]
    size = out_refs[0].shape[0]
    for i, out in enumerate(out_refs):
        rows = slice(i * size, (i + 1) * size)
        total = refs[0][rows, :].astype(f32)
        for ref in refs[1:terms]:
            total = total + ref[rows, :].astype(f32)
        out[...] = total.astype(out.dtype)


def run_add(values, pieces, kind):
    rows, width = values[0].shape
    tile = width // 2 if rows * width > 65536 and width % 256 == 0 else width
    spec = lambda size: pl.BlockSpec((size, tile), lambda j: (0, j))
    size = rows // pieces
    return pl.pallas_call(
        functools.partial(add_kernel, len(values)),
        grid=(width // tile,),
        in_specs=[spec(rows)] * len(values),
        out_specs=[spec(size)] * pieces,
        out_shape=[jax.ShapeDtypeStruct((size, width), kind)] * pieces,
        compiler_params=pltpu.CompilerParams(vmem_limit_bytes=VMEM_LIMIT),
        cost_estimate=LIGHT,
        name="add_parts",
    )(*values)


def mixed_kernel(full, terms, sq_ref, x_ref, *refs):
    length = x_ref.shape[0]
    inv = lax.rsqrt(token_column(sq_ref, pl.program_id(0), length)[:, :1] / full + epsilon)
    total = refs[0][...].astype(f32)
    for ref in refs[1:terms]:
        total = total + ref[...].astype(f32)
    refs[terms][...] = (x_ref[...].astype(f32) + inv * total).astype(bf16)


def run_mixed(squares, x_in, values, full):
    tokens, features = x_in.shape
    blocks, length = squares.shape
    rows = pl.BlockSpec((length, features), lambda b: (b, 0))
    return pl.pallas_call(
        functools.partial(mixed_kernel, full, len(values)),
        grid=(blocks,),
        in_specs=[pl.BlockSpec((blocks, length), lambda b: (0, 0)), rows] + [rows] * len(values),
        out_specs=rows,
        out_shape=jax.ShapeDtypeStruct((tokens, features), bf16),
        compiler_params=pltpu.CompilerParams(vmem_limit_bytes=VMEM_LIMIT),
        cost_estimate=LIGHT,
        name="layer_output",
    )(squares, x_in, *values)


def finish_kernel(terms, x_ref, cot_ref, inv_ref, gain_ref, *refs):
    x = x_ref[...].astype(f32)
    inv = inv_ref[...]
    total = refs[0][...].astype(f32)
    for ref in refs[1:terms]:
        total = total + ref[...].astype(f32)
    gained = total * gain_ref[...]
    spread = inv * inv * inv * jnp.sum(gained * x, axis=1, keepdims=True) / x.shape[1]
    refs[-1][...] = (cot_ref[...].astype(f32) + inv * gained - x * spread).astype(bf16)


def run_finish(values, x_in, cotangent, inv_rms, norm_gain, length):
    tokens, features = x_in.shape
    rows = lambda width: pl.BlockSpec((length, width), lambda b: (b, 0))
    return pl.pallas_call(
        functools.partial(finish_kernel, len(values)),
        grid=(tokens // length,),
        in_specs=[rows(features), rows(features), rows(1), pl.BlockSpec((1, features), lambda b: (0, 0))]
        + [rows(features)] * len(values),
        out_specs=rows(features),
        out_shape=jax.ShapeDtypeStruct((tokens, features), bf16),
        compiler_params=pltpu.CompilerParams(vmem_limit_bytes=VMEM_LIMIT),
        cost_estimate=LIGHT,
        name="input_grad_finish",
    )(x_in, cotangent, inv_rms, norm_gain[None], *values)


def over_columns(left, right):
    return lax.dot_general(left, right, (((1,), (1,)), ((), ())), preferred_element_type=f32)


def after(value, *others):
    return lax.optimization_barrier((value,) + others)[0]


def from_side(value):
    return lax.ppermute(value, "tensor", [(0, 1), (1, 0)])


def side_start(value):
    if lax.axis_size("tensor") == 2:
        return value, from_side(value)
    return None, lax.psum(value, "tensor")


def present(pair):
    return [value for value in pair if value is not None]


def side_total(pair):
    value, got = pair
    return got.astype(f32) if value is None else value.astype(f32) + got.astype(f32)


def pair_up(value, bit):
    size = lax.axis_size("dp")
    return lax.ppermute(value, "dp", [(i, i ^ bit) for i in range(size)])


def dealt_order(bits):
    order = [0]
    for bit in reversed(bits):
        order = order + [j | bit for j in order]
    return order


class Order:
    def __init__(self):
        self.pending = []

    def first(self, value):
        return after(value, *self.pending) if self.pending else value

    def then(self, value):
        self.pending = [value]
        return value

    def wait(self, value):
        self.pending = self.pending + [value]


def send_pieces(pieces, bit):
    return pieces[0], pair_up(pieces[1], bit)


def add_all(order, sent, kind=bf16):
    kept, got = sent
    return order.then(run_add([order.first(kept), got], 1, kind)[0])


def add_send(order, sent, bit):
    kept, got = sent
    pieces = run_add([order.first(kept), got], 2, bf16)
    order.then(pieces[0])
    return send_pieces(pieces, bit)


def add_last(order, sent, bits):
    for bit in bits:
        sent = add_send(order, sent, bit)
    return add_all(order, sent)


def send_same(value, bit):
    return value, pair_up(value, bit)


def local(
    x_in,
    norm_gain,
    w_zx,
    w_bc,
    w_dt,
    conv_x,
    conv_bc,
    dt_bias,
    a_log,
    d_skip,
    gate_gain,
    w_out,
    cotangent,
    block_parent,
):
    tokens, features = x_in.shape
    heads = w_dt.shape[1]
    inner = w_zx.shape[2]
    head_dim = inner // heads
    sides = lax.axis_size("tensor")
    dp = lax.axis_size("dp")
    full = inner * sides
    blocks = block_parent.shape[0]
    length = tokens // blocks
    wide = w_bc.shape[1]
    small = -(-(wide + heads) // 128) * 128
    window = conv_x.shape[0] - 1
    share = features // dp
    me = lax.axis_index("dp")

    near = []
    bit = 2
    while bit < dp:
        near.append(bit)
        bit *= 2
    far = near[1:] + near[:1]

    def places(bits):
        return lax.bitwise_xor(me, jnp.asarray(dealt_order(bits), jnp.int32)).astype(jnp.int32)

    place_near, place_far = places(near), places(far)

    head_of = jnp.arange(inner, dtype=jnp.int32) // head_dim
    one_hot = (jnp.arange(heads, dtype=jnp.int32)[:, None] == head_of[None, :]).astype(bf16)
    sel = jnp.concatenate([one_hot, one_hot], axis=0)
    sel_t = (jnp.arange(128, dtype=jnp.int32)[None, :] == head_of[:, None]).astype(bf16)
    skip_l = jnp.repeat(d_skip, head_dim)[None]

    count = blocks // 2
    step = count * length
    w_dt_t = w_dt.T
    join = lambda values: jnp.concatenate(values, axis=0)

    order = Order()
    normed, turned, inv_rms, bc_pre, dt_raw = run_norm(x_in, cotangent, norm_gain, w_bc, w_dt_t, length)
    turned_near = pair_up(turned, 1)
    w_cat = w_zx.reshape(features, 2 * inner)
    zx = jnp.dot(normed, w_cat, preferred_element_type=f32).astype(bf16)
    dgn = over_columns(after(cotangent, zx), w_out).astype(bf16)
    y, xc, pre, gg, bcc, bcp, hs, sq = run_forward(
        block_parent, bc_pre, dt_raw, zx, dgn, conv_x, conv_bc, dt_bias, a_log, skip_l, gate_gain, sel
    )
    sums = side_start(join([sq[:, 0, :], sq[:, 8, :]]))
    out = jnp.dot(gg, w_out, preferred_element_type=f32).astype(bf16)
    sums = side_total((None if sums[0] is None else after(sums[0], out), sums[1]))
    gg_near = pair_up(gg, 1)
    got_out = side_start(after(out, sums))
    squares, crosses = sums[:blocks], sums[blocks:]
    inv_gate = lax.rsqrt(squares / full + epsilon)
    scale = inv_gate.reshape(1, tokens)
    scale = jnp.concatenate([scale, pair_up(scale, 1)], axis=1)
    dz, dy, gg_grad = run_ungate(squares, crosses, y, zx, dgn, gate_gain, full)
    order.then(dz)
    dz_near = pair_up(dz, 1)
    rights = [order.first(gg), gg_near]
    pieces = run_grad(place_near, 1, turned, turned_near, rights, share, 0, inner, 2, scale)
    order.then(pieces[0])
    w_out_1 = send_pieces(pieces, near[0])
    rights = [order.first(dz), dz_near]
    pieces = run_grad(place_near, 0, turned, turned_near, rights, share, 0, inner, 2)
    order.then(pieces[0])
    w_z_1 = send_pieces(pieces, near[0])

    tail = (conv_x, conv_bc, dt_bias, a_log, skip_l, sel, sel_t, small)
    back = run_backward(
        0, blocks, block_parent, order.first(dy), xc, pre, zx, hs, bcc, bcp, bc_pre, dt_raw, *tail, ()
    )
    dx, dbc, ddt, gkx, gkbc, gskip, ghead = back
    order.then(dx)
    order.wait(got_out[1])
    order.wait(w_out_1[1])
    w_out_2 = add_send(order, w_out_1, near[1])
    dx_near = pair_up(dx, 1)
    got_bc = side_start(dbc)
    low, low_gain = run_input(dz, order.first(dx), dbc, ddt, w_cat, w_bc, w_dt_t, x_in, inv_rms, 0, tokens)
    order.then(low)
    got_low = side_start(low)
    order.wait(w_z_1[1])
    w_out_3 = add_send(order, w_out_2, near[2])
    w_z_2 = add_send(order, w_z_1, near[1])
    got_bc = tuple(None if value is None else order.first(value) for value in got_bc)
    d_small = jnp.concatenate([side_total(got_bc).astype(bf16), ddt], axis=1)
    order.then(d_small)
    small_near = pair_up(d_small, 1)
    edge = inner * 5 // 8 // 256 * 256
    pieces = run_grad(place_near, 0, turned, turned_near, [order.first(dx), dx_near], share, 0, edge, 2)
    order.then(pieces[1])
    sent_a = send_pieces(pieces, near[0])
    pieces = run_grad(place_near, 0, turned, turned_near, [order.first(d_small), small_near], share, 0, small, 2)
    order.then(pieces[1])
    sent_s = send_pieces(pieces, near[0])
    pieces = run_grad(place_far, 0, turned, turned_near, [order.first(dx), dx_near], share, edge, inner - edge, 2)
    order.then(pieces[1])
    w_out_grad = add_last(order, w_out_3, near[3:])
    sent_b = send_pieces(pieces, far[0])

    def spread_rows(sent, bit):
        kept, got = sent
        places_s.extend([j ^ bit for j in places_s])
        return order.then(join([order.first(kept), got]))

    places_s = [0]
    sent_a = add_send(order, sent_a, near[1])
    sent_s = add_send(order, sent_s, near[1])
    w_z_3 = add_send(order, w_z_2, near[2])
    mixed = order.then(run_mixed(squares, order.first(x_in), present(got_out), full))
    low_gain, gkbc, gskip, gkx, ghead, gg_grad = order.first((low_gain, gkbc, gskip, gkx, ghead, gg_grad))
    shared = jnp.concatenate([low_gain.reshape(-1), gkbc.reshape(-1)])
    d_skip_part = jnp.sum(gskip.reshape(heads, head_dim), axis=1)
    own = jnp.concatenate(
        [gkx.reshape(-1), ghead.reshape(-1), d_skip_part, gg_grad.reshape(-1)]
    )
    n_shared, n_own = shared.shape[0], own.shape[0]
    pad_shared = -(-n_shared // 1024) * 1024
    pad_own = -(-n_own // 1024) * 1024
    shared = jnp.concatenate([shared, jnp.zeros((pad_shared - n_shared,), f32)]).reshape(-1, 128)
    own = jnp.concatenate([own, jnp.zeros((pad_own - n_own,), f32)]).reshape(-1, 128)
    packed = join([shared, own])

    order.then(packed)
    packed = send_same(packed, 1)
    sent_b = add_send(order, sent_b, far[1])
    packed = send_same(add_all(order, packed, f32), near[0])
    sent_a = add_send(order, sent_a, near[2])
    sent_s = add_send(order, sent_s, near[2])
    packed = send_same(add_all(order, packed, f32), near[1])
    w_z_grad = add_last(order, w_z_3, near[3:])
    w_s = add_last(order, sent_s, near[3:])
    rows_bc = send_same(w_s[:, :wide], near[2])
    sent_b = add_send(order, sent_b, far[2])
    packed = send_same(add_all(order, packed, f32), near[2])
    rows_bc = send_same(spread_rows(rows_bc, near[2]), near[1])
    w_x_a = add_last(order, sent_a, near[3:])
    packed = add_all(order, packed, f32)
    for bit in near[3:]:
        packed = add_all(order, send_same(packed, bit), f32)
    got_shared = side_start(packed[: pad_shared // 128])
    rows_bc = send_same(spread_rows(rows_bc, near[1]), near[0])
    values = present(got_low)
    input_grad = order.then(
        run_finish([order.first(values[0])] + values[1:], x_in, cotangent, inv_rms, norm_gain, length)
    )
    w_x_b = add_last(order, sent_b, far[3:])
    rows_bc = spread_rows(rows_bc, near[0])
    for bit in near[3:]:
        rows_bc = spread_rows(send_same(rows_bc, bit), bit)
    rows_bc = spread_rows(send_same(rows_bc, 1), 1)
    chunks = rows_bc.reshape(dp, share, wide)
    back_to = jnp.asarray([places_s.index(j) for j in range(dp)], jnp.int32)
    w_bc_grad = jnp.take(chunks, back_to[lax.bitwise_xor(me, jnp.arange(dp, dtype=jnp.int32))], axis=0)
    w_bc_grad = w_bc_grad.reshape(features, wide).astype(f32)
    w_dt_grad = w_s[:, wide : wide + heads].astype(f32)
    w_x_grad = jnp.concatenate([w_x_a, w_x_b], axis=1)
    shared = side_total(got_shared).reshape(-1)
    own = packed[pad_shared // 128 :].reshape(-1)

    edge = (window + 1) * inner
    w_zx_grad = jnp.stack([w_z_grad, w_x_grad], axis=1).astype(f32)
    return (
        mixed,
        input_grad,
        shared[:features],
        w_zx_grad,
        w_bc_grad,
        w_dt_grad,
        own[:edge].reshape(window + 1, inner),
        shared[features:n_shared].reshape(window + 1, wide),
        own[edge : edge + heads],
        own[edge + heads : edge + 2 * heads],
        own[edge + 2 * heads : edge + 3 * heads],
        own[edge + 3 * heads : n_own],
        w_out_grad.astype(f32).T,
    )


def solution(mesh):
    return jax.shard_map(
        local,
        mesh=mesh,
        in_specs=(
            P("dp", None),
            P(),
            P(None, None, "tensor"),
            P(),
            P(None, "tensor"),
            P(None, "tensor"),
            P(),
            P("tensor"),
            P("tensor"),
            P("tensor"),
            P("tensor"),
            P("tensor", None),
            P("dp", None),
            P("dp"),
        ),
        out_specs=(
            P("dp", None),
            P("dp", None),
            P(),
            P("dp", None, "tensor"),
            P(),
            P("dp", "tensor"),
            P(None, "tensor"),
            P(),
            P("tensor"),
            P("tensor"),
            P("tensor"),
            P("tensor"),
            P("tensor", "dp"),
        ),
        check_vma=False,
    )
```

```python
import functools

import jax
import jax.numpy as jnp
from jax import lax
from jax.experimental import pallas as pl
from jax.experimental.pallas import tpu as pltpu
from jax.sharding import PartitionSpec as P

epsilon = 1e-05
f32 = jnp.float32
bf16 = jnp.bfloat16
VMEM_LIMIT = 60 * 1024 * 1024
LIGHT = pl.CostEstimate(flops=1000, bytes_accessed=1000, transcendentals=0)


def sigmoid(v):
    return 0.5 * jnp.tanh(0.5 * v) + 0.5


def dot(a, b, dims=((1,), (0,)), precision=None):
    return lax.dot_general(a, b, (dims, ((), ())), precision=precision, preferred_element_type=f32)


NN = ((1,), (0,))
NT = ((1,), (1,))
TN = ((0,), (0,))
highest = lax.Precision.HIGHEST


def split_low(v):
    hi = v.astype(bf16)
    lo = (v - hi.astype(f32)).astype(bf16)
    return hi, lo


def head_masks(length, head_dim):
    lane = lax.broadcasted_iota(jnp.int32, (length, 2 * head_dim), 1)
    return lane < head_dim


def pair_stack(v, first):
    zero = jnp.zeros_like(v)
    return jnp.concatenate([jnp.where(first, v, zero), jnp.where(first, zero, v)], axis=0)


def tri_mask(length):
    row = lax.broadcasted_iota(jnp.int32, (length, length), 0)
    col = lax.broadcasted_iota(jnp.int32, (length, length), 1)
    return row, col


def step_values(dtr_ref, bias_ref, alog_ref, length):
    row, col = tri_mask(length)
    dtr = dtr_ref[...] + bias_ref[...]
    dt = jnp.maximum(dtr, 0.0) + jnp.log1p(jnp.exp(-jnp.abs(dtr)))
    rate = -jnp.exp(alog_ref[...])
    tri = (row >= col).astype(f32)
    cum = dot(tri, dt * rate, NN, highest)
    last = cum[length - 1 : length, :]
    return dtr, dt, rate, cum, jnp.exp(cum), jnp.exp(jnp.minimum(last - cum, 0.0))


def store_columns(cum, cum_s, cumt_s, heads):
    cum_s[:, :heads] = cum
    cumt_s[...] = jnp.transpose(cum_s[...])


def conv_rows(ext, kern, length, window):
    base = ext.shape[0] - length - (window - 1)
    total = kern[window : window + 1, :] + kern[window - 1 : window, :] * ext[ext.shape[0] - length :, :]
    for offset in range(window - 1):
        total = total + kern[offset : offset + 1, :] * ext[base + offset : base + offset + length, :]
    return total


def forward_kernel(
    sizes,
    par_ref,
    bc_ref,
    dtr_ref,
    z_ref,
    xp_ref,
    dgn_ref,
    kx_ref,
    kbc_ref,
    bias_ref,
    alog_ref,
    skip_ref,
    gain_ref,
    sel_ref,
    y_ref,
    xc_ref,
    pre_ref,
    gg_ref,
    bcc_ref,
    bcp_ref,
    hs_ref,
    sq_ref,
    h_end,
    tail_x,
    tail_bc,
    lhs_s,
    cum_s,
    cumt_s,
    score_s,
    acc_s,
    cross_s,
):
    length, inner, heads, head_dim, lanes, blocks, window = sizes
    state = bcc_ref.shape[1] // 2
    b = pl.program_id(0)
    par = par_ref[b]
    slot = jnp.where(par >= 0, par, blocks)

    @pl.when(b == 0)
    def _():
        h_end[blocks] = jnp.zeros(h_end.shape[1:], f32)
        tail_x[blocks] = jnp.zeros(tail_x.shape[1:], f32)
        tail_bc[blocks] = jnp.zeros(tail_bc.shape[1:], f32)
        cum_s[...] = jnp.zeros_like(cum_s)

    bcv = bc_ref[...]
    pre = conv_rows(jnp.concatenate([tail_bc[slot], bcv], axis=0), kbc_ref[...], length, window)
    tail_bc[b] = bcv[length - 8 :, :]
    bcc = (pre * sigmoid(pre)).astype(bf16)
    bcc_ref[...] = bcc
    bcp_ref[...] = pre
    c_rows = bcc[:, state:]
    b_rows = bcc[:, :state]
    row, col = tri_mask(length)
    score_s[...] = jnp.where(row >= col, dot(c_rows, b_rows, NT), 0.0)

    _, dt, _, cum, from_start, to_end = step_values(dtr_ref, bias_ref, alog_ref, length)
    hi, lo = split_low(jnp.concatenate([dt, from_start, to_end], axis=0))
    lhs_s[...] = jnp.concatenate([hi, lo], axis=1)
    store_columns(cum, cum_s, cumt_s, heads)
    acc_s[...] = jnp.zeros_like(acc_s)
    cross_s[...] = jnp.zeros_like(cross_s)
    first = head_masks(length, head_dim)
    group = lanes // head_dim
    pair = 2 * head_dim

    def body(g, carry):
        sl = pl.ds(pl.multiple_of(g * lanes, lanes), lanes)
        xpv = xp_ref[:, sl].astype(f32)
        ext = jnp.concatenate([tail_x[slot, :, sl], xpv], axis=0)
        pre_x = conv_rows(ext, kx_ref[:, sl], length, window)
        tail_x[b, :, sl] = xpv[length - 8 :, :]
        xc = (pre_x * sigmoid(pre_x)).astype(bf16)
        pre_ref[:, sl] = pre_x.astype(bf16)
        xc_ref[:, sl] = xc
        wide = dot(lhs_s[...], sel_ref[:, sl])
        dt_l = wide[:length]
        start_l = wide[length : 2 * length]
        end_l = wide[2 * length :]
        xcf = xc.astype(f32)
        xd = dt_l * xcf
        xdb = xd.astype(bf16)
        gx = (end_l * xd).astype(bf16)
        h = h_end[slot, :, sl]
        hb = h.astype(bf16)
        hs_ref[0, :, sl] = hb
        carried = start_l * dot(c_rows, hb)
        h_end[b, :, sl] = start_l[length - 1 : length, :] * h + dot(b_rows, gx, TN)
        cols = pltpu.roll(cum_s[...], cum_s.shape[1] - g * group, 1)
        rows = cumt_s[pl.ds(pl.multiple_of(g * group, 8), max(group, 8)), :]
        score = score_s[...]
        skip = skip_ref[:, sl]
        gain = gain_ref[:, sl]
        zv = z_ref[:, sl].astype(f32)
        gate = zv * sigmoid(zv)
        acc = acc_s[...]
        cross = cross_s[...]
        dgn = dgn_ref[:, sl].astype(f32)
        for q in range(lanes // pair):
            at = slice(q * pair, (q + 1) * pair)
            weights = []
            for h_at in (2 * q, 2 * q + 1):
                gap = jnp.minimum(cols[:, h_at : h_at + 1] - rows[h_at : h_at + 1, :], 0.0)
                weights.append((score * jnp.exp(gap)).astype(bf16))
            within = dot(jnp.concatenate(weights, axis=1), pair_stack(xdb[:, at], first))
            y = (within + carried[:, at] + skip[:, at] * xcf[:, at]).astype(bf16)
            out = pl.ds(pl.multiple_of(g * lanes + q * pair, pair), pair)
            y_ref[:, out] = y
            gated = y.astype(f32) * gate[:, at]
            gained = gated * gain[:, at]
            gg_ref[:, out] = gained.astype(bf16)
            acc = acc + gated * gated
            cross = cross + dgn[:, at] * gained
        acc_s[...] = acc
        cross_s[...] = cross
        return carry

    lax.fori_loop(0, inner // lanes, body, 0)
    ones = jnp.ones((8, pair), f32)
    sq_ref[0, :8, :] = dot(ones, acc_s[...], NT, highest)
    sq_ref[0, 8:, :] = dot(ones, cross_s[...], NT, highest)


def run_forward(parent, bc_pre, dt_raw, zx, dgn, conv_x, conv_bc, dt_bias, a_log, skip_l, gate_gain, sel):
    tokens = zx.shape[0]
    inner = conv_x.shape[1]
    heads = dt_raw.shape[1]
    head_dim = inner // heads
    blocks = parent.shape[0]
    length = tokens // blocks
    window = conv_x.shape[0] - 1
    wide = bc_pre.shape[1]
    state = wide // 2
    lanes = min(512, inner)
    sizes = (length, inner, heads, head_dim, lanes, blocks, window)
    whole = lambda shape: pl.BlockSpec(shape, lambda b, *_: (0,) * len(shape))
    rows = lambda width: pl.BlockSpec((length, width), lambda b, *_: (b, 0))
    block = lambda shape: pl.BlockSpec((1,) + shape, lambda b, *_: (b, 0, 0))
    grid_spec = pltpu.PrefetchScalarGridSpec(
        num_scalar_prefetch=1,
        grid=(blocks,),
        in_specs=[
            rows(wide),
            rows(heads),
            rows(inner),
            pl.BlockSpec((length, inner), lambda b, *_: (b, 1)),
            rows(inner),
            whole(conv_x.shape),
            whole(conv_bc.shape),
            whole((1, heads)),
            whole((1, heads)),
            whole((1, inner)),
            whole((1, inner)),
            whole(sel.shape),
        ],
        out_specs=[
            rows(inner),
            rows(inner),
            rows(inner),
            rows(inner),
            rows(wide),
            rows(wide),
            block((state, inner)),
            block((16, length)),
        ],
        scratch_shapes=[
            pltpu.VMEM((blocks + 1, state, inner), f32),
            pltpu.VMEM((blocks + 1, 8, inner), f32),
            pltpu.VMEM((blocks + 1, 8, wide), f32),
            pltpu.VMEM((3 * length, 2 * heads), bf16),
            pltpu.VMEM((length, length), f32),
            pltpu.VMEM((length, length), f32),
            pltpu.VMEM((length, length), f32),
            pltpu.VMEM((length, 2 * head_dim), f32),
            pltpu.VMEM((length, 2 * head_dim), f32),
        ],
    )
    return pl.pallas_call(
        functools.partial(forward_kernel, sizes),
        grid_spec=grid_spec,
        out_shape=[jax.ShapeDtypeStruct((tokens, inner), bf16)] * 4
        + [
            jax.ShapeDtypeStruct((tokens, wide), bf16),
            jax.ShapeDtypeStruct((tokens, wide), f32),
            jax.ShapeDtypeStruct((blocks, state, inner), bf16),
            jax.ShapeDtypeStruct((blocks, 16, length), f32),
        ],
        compiler_params=pltpu.CompilerParams(vmem_limit_bytes=VMEM_LIMIT),
        cost_estimate=LIGHT,
        name="ssd_forward",
    )(parent, bc_pre, dt_raw, zx, zx, dgn, conv_x, conv_bc, dt_bias[None], a_log[None], skip_l, gate_gain[None], sel)


def token_column(row_ref, at, length):
    row = row_ref[pl.ds(at, 1), :]
    return jnp.transpose(jnp.broadcast_to(row, (length, length)))


def ungate_kernel(sizes, sq_ref, cross_ref, y_ref, z_ref, dgn_ref, gain_ref, dz_ref, dy_ref, grad_ref):
    length, inner, lanes, full = sizes
    b = pl.program_id(0)
    inv = lax.rsqrt(token_column(sq_ref, b, length) / full + epsilon)
    coef = inv * token_column(cross_ref, b, length) / full

    @pl.when(b == 0)
    def _():
        grad_ref[...] = jnp.zeros_like(grad_ref)

    def body(g, carry):
        sl = pl.ds(pl.multiple_of(g * length, length), length)
        zv = z_ref[:, sl].astype(f32)
        sig = sigmoid(zv)
        gate = zv * sig
        gain = gain_ref[:, sl]
        y = y_ref[:, sl].astype(f32) * inv
        scaled = y * gate
        dgn = dgn_ref[:, sl].astype(f32)
        grad_ref[:, sl] += jnp.sum(dgn * scaled, axis=0, keepdims=True)
        d_scaled = dgn * gain - scaled * coef
        dz_ref[:, sl] = (d_scaled * y * (sig + gate * (1.0 - sig))).astype(bf16)
        dy_ref[:, sl] = (d_scaled * inv * gate).astype(bf16)
        return carry

    lax.fori_loop(0, inner // length, body, 0, unroll=2)


def run_ungate(squares, cross, y, zx, dgn, gate_gain, full):
    tokens, inner = y.shape
    blocks, length = squares.shape
    rows = pl.BlockSpec((length, inner), lambda b: (b, 0))
    one = pl.BlockSpec((1, inner), lambda b: (0, 0))
    small = pl.BlockSpec((blocks, length), lambda b: (0, 0))
    return pl.pallas_call(
        functools.partial(ungate_kernel, (length, inner, length, full)),
        grid=(blocks,),
        in_specs=[small, small, rows, rows, rows, one],
        out_specs=[rows, rows, one],
        out_shape=[jax.ShapeDtypeStruct((tokens, inner), bf16)] * 2 + [jax.ShapeDtypeStruct((1, inner), f32)],
        compiler_params=pltpu.CompilerParams(vmem_limit_bytes=VMEM_LIMIT),
        cost_estimate=LIGHT,
        name="gate_backward",
    )(squares, cross, y, zx, dgn, gate_gain[None])


def norm_kernel(features, x_ref, cot_ref, gain_ref, wbc_ref, wdt_ref, normed_ref, turned_ref, inv_ref, bc_ref, dtr_ref):
    x = x_ref[...].astype(f32)
    inv = lax.rsqrt(jnp.sum(x * x, axis=1, keepdims=True) / features + epsilon)
    inv_ref[...] = inv
    normed = (x * inv * gain_ref[...]).astype(bf16)
    normed_ref[...] = normed
    turned_ref[0] = jnp.transpose(normed)
    turned_ref[1] = jnp.transpose(cot_ref[...])
    bc_ref[...] = dot(normed, wbc_ref[...])
    dtr_ref[...] = dot(normed, wdt_ref[...], NT)


def run_norm(x_in, cotangent, norm_gain, w_bc, w_dt_t, length):
    tokens, features = x_in.shape
    wide = w_bc.shape[1]
    heads = w_dt_t.shape[0]
    rows = lambda width: pl.BlockSpec((length, width), lambda b: (b, 0))
    whole = lambda shape: pl.BlockSpec(shape, lambda b: (0, 0), pipeline_mode=pl.Buffered(1))
    turned = pl.BlockSpec((2, features, length), lambda b: (0, 0, b))
    return pl.pallas_call(
        functools.partial(norm_kernel, features),
        grid=(tokens // length,),
        in_specs=[rows(features), rows(features), whole((1, features)), whole(w_bc.shape), whole(w_dt_t.shape)],
        out_specs=[rows(features), turned, rows(1), rows(wide), rows(heads)],
        out_shape=[
            jax.ShapeDtypeStruct((tokens, features), bf16),
            jax.ShapeDtypeStruct((2, features, tokens), bf16),
            jax.ShapeDtypeStruct((tokens, 1), f32),
            jax.ShapeDtypeStruct((tokens, wide), f32),
            jax.ShapeDtypeStruct((tokens, heads), f32),
        ],
        compiler_params=pltpu.CompilerParams(vmem_limit_bytes=VMEM_LIMIT),
        cost_estimate=LIGHT,
        name="input_norm",
    )(x_in, cotangent, norm_gain[None], w_bc, w_dt_t)


def fetch_left(share, which, place_ref, mine_ref, theirs_ref, left_s, sem):
    tokens = mine_ref.shape[2]
    count = left_s.shape[0] // share
    copies = []
    for i in range(count):
        src = pl.ds(pl.multiple_of(place_ref[i] * share, share), share)
        for side, ref in enumerate((mine_ref, theirs_ref)):
            copies.append(
                pltpu.make_async_copy(
                    ref.at[which, src, :],
                    left_s.at[pl.ds(i * share, share), pl.ds(side * tokens, tokens)],
                    sem.at[2 * i + side],
                )
            )
    return copies


def gather_right(refs, right_s):
    at = 0
    for ref in refs:
        size = ref.shape[0]
        right_s[at : at + size, :] = ref[...]
        at += size


def load_left(share, which, place_ref, mine_ref, theirs_ref, left_s, sem):
    copies = fetch_left(share, which, place_ref, mine_ref, theirs_ref, left_s, sem)
    for copy in copies:
        copy.start()
    for copy in copies:
        copy.wait()


def grad_kernel(share, which, pieces, scaled, outs, place_ref, mine_ref, theirs_ref, *rest):
    rights = rest[:pieces]
    rest = rest[pieces:]
    if scaled:
        scale_ref = rest[0]
        rest = rest[1:]
    out_refs = rest[:outs]
    left_s, right_s, sem = rest[outs:]

    @pl.when(pl.program_id(0) == 0)
    def _():
        load_left(share, which, place_ref, mine_ref, theirs_ref, left_s, sem)
        if scaled:
            rows_at = left_s.shape[0] // 8

            def apply(i, carry):
                at = pl.ds(pl.multiple_of(i * rows_at, rows_at), rows_at)
                left_s[at, :] = (left_s[at, :].astype(f32) * scale_ref[...]).astype(bf16)
                return carry

            lax.fori_loop(0, 8, apply, 0)

    gather_right(rights, right_s)
    total = dot(left_s[...], right_s[...])
    size = out_refs[0].shape[0]
    for i, ref in enumerate(out_refs):
        ref[...] = total[i * size : (i + 1) * size].astype(bf16)


def run_grad(places, which, mine, theirs, rights, share, first, width, outs, scale=None):
    tokens = mine.shape[2]
    count = places.shape[0]
    rows = count * share
    tile = 256 if width % 256 == 0 and first % 256 == 0 else 128
    anywhere = pl.BlockSpec(memory_space=pl.ANY)
    columns = [
        pl.BlockSpec((right.shape[0], tile), lambda j, *_: (0, first // tile + j)) for right in rights
    ]
    extra = [] if scale is None else [pl.BlockSpec(scale.shape, lambda j, *_: (0, 0))]
    return pl.pallas_call(
        functools.partial(grad_kernel, share, which, len(rights), scale is not None, outs),
        grid_spec=pltpu.PrefetchScalarGridSpec(
            num_scalar_prefetch=1,
            grid=(width // tile,),
            in_specs=[anywhere, anywhere] + columns + extra,
            out_specs=[pl.BlockSpec((rows // outs, tile), lambda j, *_: (0, j))] * outs,
            scratch_shapes=[
                pltpu.VMEM((rows, 2 * tokens), bf16),
                pltpu.VMEM((2 * tokens, tile), bf16),
                pltpu.SemaphoreType.DMA((2 * count,)),
            ],
        ),
        out_shape=[jax.ShapeDtypeStruct((rows // outs, width), bf16)] * outs,
        compiler_params=pltpu.CompilerParams(vmem_limit_bytes=VMEM_LIMIT),
        cost_estimate=LIGHT,
        name="weight_grad",
    )(places, mine, theirs, *rights, *([] if scale is None else [scale]))


def input_kernel(heads, dz_ref, dx_ref, dbc_ref, ddt_ref, wz_ref, wx_ref, wbc_ref, wdt_ref, x_ref, inv_ref, out_ref, gain_ref):
    total = dot(dz_ref[...], wz_ref[...], NT) + dot(dx_ref[...], wx_ref[...], NT)
    total = total + dot(dbc_ref[...], wbc_ref[...], NT)
    total = total + dot(ddt_ref[:, :heads], wdt_ref[...], NN)
    out_ref[...] = total.astype(bf16)
    gain_ref[...] = jnp.sum(total * (x_ref[...].astype(f32) * inv_ref[...]), axis=0, keepdims=True)


def run_input(dz, dx, dbc, ddt, w_cat, w_bc, w_dt_t, x_in, inv_rms, at, tokens):
    inner = dz.shape[1]
    features = x_in.shape[1]
    wide = w_bc.shape[1]
    heads = w_dt_t.shape[0]
    tile = 256
    side = lambda width: pl.BlockSpec((tokens, width), lambda j: (at, 0), pipeline_mode=pl.Buffered(1))
    return pl.pallas_call(
        functools.partial(input_kernel, heads),
        grid=(features // tile,),
        in_specs=[
            side(inner),
            side(inner),
            side(wide),
            side(ddt.shape[1]),
            pl.BlockSpec((tile, inner), lambda j: (j, 0)),
            pl.BlockSpec((tile, inner), lambda j: (j, 1)),
            pl.BlockSpec((tile, wide), lambda j: (j, 0)),
            pl.BlockSpec((heads, tile), lambda j: (0, j)),
            pl.BlockSpec((tokens, tile), lambda j: (at, j)),
            pl.BlockSpec((tokens, 1), lambda j: (at, 0)),
        ],
        out_specs=[pl.BlockSpec((tokens, tile), lambda j: (0, j)), pl.BlockSpec((1, tile), lambda j: (0, j))],
        out_shape=[jax.ShapeDtypeStruct((tokens, features), bf16), jax.ShapeDtypeStruct((1, features), f32)],
        compiler_params=pltpu.CompilerParams(vmem_limit_bytes=VMEM_LIMIT),
        cost_estimate=pl.CostEstimate(flops=27 * 900_000_000, bytes_accessed=1000, transcendentals=0),
        name="input_grad",
    )(dz, dx, dbc, ddt, w_cat, w_cat, w_bc, w_dt_t, x_in, inv_rms)


def conv_back(ext, kern, inputs, length, window):
    total = kern[window - 1 : window, :] * ext[:length, :]
    sums = [None] * (window + 1)
    sums[window] = jnp.sum(ext[:length, :], axis=0, keepdims=True)
    sums[window - 1] = jnp.sum(inputs * ext[:length, :], axis=0, keepdims=True)
    for shift in range(1, window):
        moved = ext[shift : shift + length, :]
        total = total + kern[window - 1 - shift : window - shift, :] * moved
        sums[window - 1 - shift] = jnp.sum(inputs * moved, axis=0, keepdims=True)
    return total, jnp.concatenate(sums, axis=0)


def backward_kernel(
    sizes,
    par_ref,
    dy_ref,
    xc_ref,
    pre_ref,
    xp_ref,
    hs_ref,
    bcc_ref,
    bcp_ref,
    bc_ref,
    dtr_ref,
    kx_ref,
    kbc_ref,
    bias_ref,
    alog_ref,
    skip_ref,
    sel_ref,
    selt_ref,
    *rest,
):
    length, inner, heads, head_dim, lanes, blocks, window, start, count = sizes
    last_chunk = start + count == blocks
    if not last_chunk:
        ds_prev, nx_prev, nbc_prev = rest[:3]
        rest = rest[3:]
    dxp_ref, dbc_ref, ddt_ref, gkx_ref, gkbc_ref, gskip_ref, ghead_ref = rest[:7]
    rest = rest[7:]
    if start:
        ds_next, nx_next, nbc_next = rest[:3]
        rest = rest[3:]
    (
        d_state,
        next_x,
        next_bc,
        lhs_s,
        cum_s,
        cumt_s,
        score_s,
        dscore_s,
        db_s,
        dc_s,
        red_s,
        cross_s,
        inner_s,
    ) = rest
    state = bcc_ref.shape[1] // 2
    b = start + count - 1 - pl.program_id(0)
    par = par_ref[b]
    slot = jnp.where(par >= 0, par, blocks)

    @pl.when(pl.program_id(0) == 0)
    def _():
        if last_chunk:
            d_state[...] = jnp.zeros_like(d_state)
            next_x[...] = jnp.zeros_like(next_x)
            next_bc[...] = jnp.zeros_like(next_bc)
        else:
            pltpu.sync_copy(ds_prev, d_state.at[: start + count])
            next_x[: start + count] = nx_prev[...]
            next_bc[: start + count] = nbc_prev[...]
            d_state[blocks] = jnp.zeros(d_state.shape[1:], f32)
            next_x[blocks] = jnp.zeros(next_x.shape[1:], f32)
            next_bc[blocks] = jnp.zeros(next_bc.shape[1:], f32)
        cum_s[...] = jnp.zeros_like(cum_s)
        cross_s[...] = jnp.zeros_like(cross_s)
        gkx_ref[...] = jnp.zeros_like(gkx_ref)
        gkbc_ref[...] = jnp.zeros_like(gkbc_ref)
        gskip_ref[...] = jnp.zeros_like(gskip_ref)
        ghead_ref[...] = jnp.zeros_like(ghead_ref)

    bcc = bcc_ref[...]
    c_rows = bcc[:, state:]
    b_rows = bcc[:, :state]
    row, col = tri_mask(length)
    score_s[...] = jnp.where(row >= col, dot(c_rows, b_rows, NT), 0.0)
    dtr, dt, rate, cum, from_start, to_end = step_values(dtr_ref, bias_ref, alog_ref, length)
    hi, lo = split_low(jnp.concatenate([dt, from_start, to_end], axis=0))
    lhs_s[...] = jnp.concatenate([hi, lo], axis=1)
    store_columns(cum, cum_s, cumt_s, heads)
    dscore_s[...] = jnp.zeros_like(dscore_s)
    db_s[...] = jnp.zeros_like(db_s)
    dc_s[...] = jnp.zeros_like(dc_s)
    red_s[...] = jnp.zeros_like(red_s)
    first = head_masks(length, head_dim)
    group = lanes // head_dim
    pair = 2 * head_dim
    before = (row < col).astype(bf16)
    following = (row >= col).astype(f32)

    def body(g, carry):
        sl = pl.ds(pl.multiple_of(g * lanes, lanes), lanes)
        wide = dot(lhs_s[...], sel_ref[:, sl])
        dt_l = wide[:length]
        start_l = wide[length : 2 * length]
        end_l = wide[2 * length :]
        last_l = start_l[length - 1 : length, :]
        dyb = dy_ref[:, sl]
        dy = dyb.astype(f32)
        xc = xc_ref[:, sl]
        xcf = xc.astype(f32)
        xd = dt_l * xcf
        xdb = xd.astype(bf16)
        gx = (end_l * xd).astype(bf16)
        hb = hs_ref[0, :, sl]
        d_end = d_state[b, :, sl]
        d_endb = d_end.astype(bf16)
        sdy = (start_l * dy).astype(bf16)
        carried = start_l * dot(c_rows, hb)
        local = end_l * dot(b_rows, d_endb)
        dc_s[...] += dot(sdy, hb, NT)
        db_s[...] += dot(gx, d_endb, NT)
        d_state[slot, :, sl] += last_l * d_end + dot(c_rows, sdy, TN)
        carry_end = jnp.sum(d_end * hb.astype(f32), axis=0, keepdims=True) * last_l
        cols = pltpu.roll(cum_s[...], cum_s.shape[1] - g * group, 1)
        rows = cumt_s[pl.ds(pl.multiple_of(g * group, 8), max(group, 8)), :]
        score = score_s[...]
        dscore = dscore_s[...]
        crossings = []
        for q in range(lanes // pair):
            at = slice(q * pair, (q + 1) * pair)
            dy2 = pair_stack(dyb[:, at], first)
            dw2 = dot(dy2, xdb[:, at], NT)
            weights, terms = [], []
            for half in range(2):
                h_at = 2 * q + half
                gap = jnp.minimum(cols[:, h_at : h_at + 1] - rows[h_at : h_at + 1, :], 0.0)
                decay = jnp.exp(gap)
                weights.append((score * decay).astype(bf16))
                t = dw2[half * length : (half + 1) * length] * decay
                dscore = dscore + t
                terms.append((t * score).astype(bf16))
            inner_s[:, at] = dot(jnp.concatenate(weights, axis=0), dy2, TN)
            crossed = dot(jnp.concatenate(terms, axis=0), before)
            for half in range(2):
                part = crossed[half * length : (half + 1) * length] * following
                crossings.append(jnp.sum(part, axis=0, keepdims=True))
        dscore_s[...] = dscore
        cross_s[pl.ds(pl.multiple_of(g * group, 8), group), :] = jnp.concatenate(crossings, axis=0)
        dxd = inner_s[...] + local
        products = jnp.concatenate(
            [(dy * carried).astype(bf16), (local * xd).astype(bf16), (dxd * xcf).astype(bf16),
             jnp.broadcast_to(carry_end, (16, lanes)).astype(bf16)], axis=0
        )
        red_s[...] += dot(products, selt_ref[sl, :])
        gskip_ref[:, sl] += jnp.sum(dy * xcf, axis=0, keepdims=True)
        dx = dt_l * dxd + skip_ref[:, sl] * dy
        pre = pre_ref[:, sl].astype(f32)
        sig = sigmoid(pre)
        d_pre = dx * (sig + pre * sig * (1.0 - sig))
        ext = jnp.concatenate([d_pre, next_x[b, :, sl]], axis=0)
        next_x[slot, :, sl] += d_pre[:8, :]
        xpv = xp_ref[:, sl].astype(f32)
        dxp, sums = conv_back(ext, kx_ref[:, sl], xpv, length, window)
        dxp_ref[:, sl] = dxp.astype(bf16)
        gkx_ref[:, sl] += sums
        return carry

    lax.fori_loop(0, inner // lanes, body, 0)

    red = red_s[...]
    carried_t = red[:length, :heads]
    local_t = red[length : 2 * length, :heads]
    ddt = red[2 * length : 3 * length, :heads]
    end_t = red[3 * length : 3 * length + 1, :heads]
    suffix = (row <= col).astype(f32)
    prefix = (row > col).astype(f32)
    d_rate = (
        dot(suffix, carried_t, NN, highest)
        + dot(prefix, local_t, NN, highest)
        + end_t
        + jnp.transpose(cross_s[...])[:, :heads]
    )
    ddt = ddt + d_rate * rate
    ddtr = ddt * sigmoid(dtr)
    ghead_ref[0:1, :] += jnp.sum(ddtr, axis=0, keepdims=True)
    ghead_ref[1:2, :] += jnp.sum(d_rate * rate * dt, axis=0, keepdims=True)

    dscore = jnp.where(row >= col, dscore_s[...], 0.0).astype(bf16)
    d_c = dc_s[...] + dot(dscore, b_rows)
    d_b = db_s[...] + dot(dscore, c_rows, TN)
    pre = bcp_ref[...]
    sig = sigmoid(pre)
    d_pre = jnp.concatenate([d_b, d_c], axis=1) * (sig + pre * sig * (1.0 - sig))
    ext = jnp.concatenate([d_pre, next_bc[b]], axis=0)
    next_bc[slot] += d_pre[:8, :]
    dbcp, sums = conv_back(ext, kbc_ref[...], bc_ref[...], length, window)
    gkbc_ref[...] += sums
    dbc_ref[...] = dbcp.astype(bf16)
    ddt_ref[...] = jnp.zeros_like(ddt_ref)
    ddt_ref[:, :heads] = ddtr.astype(bf16)

    if start:

        @pl.when(b == start)
        def _():
            pltpu.sync_copy(d_state.at[:start], ds_next)
            nx_next[...] = next_x[:start]
            nbc_next[...] = next_bc[:start]


def run_backward(
    start, count, parent, dy, xc, pre, zx, hs, bcc, bcp, bc_pre, dt_raw, conv_x, conv_bc, dt_bias, a_log, skip_l,
    sel, sel_t, small, carry
):
    inner = conv_x.shape[1]
    heads = dt_raw.shape[1]
    head_dim = inner // heads
    blocks = parent.shape[0]
    length = dy.shape[0] // blocks
    tokens = count * length
    window = conv_x.shape[0] - 1
    wide = bcc.shape[1]
    state = wide // 2
    lanes = min(512, inner)
    anywhere = pl.BlockSpec(memory_space=pl.ANY)
    sizes = (length, inner, heads, head_dim, lanes, blocks, window, start, count)
    top = count - 1
    later = lambda width: pl.BlockSpec((length, width), lambda b, *_: (start + top - b, 0))
    whole = lambda shape: pl.BlockSpec(shape, lambda b, *_: (0,) * len(shape))
    rows = lambda width: pl.BlockSpec((length, width), lambda b, *_: (top - b, 0))
    carry_specs = [anywhere, whole(carry[1].shape), whole(carry[2].shape)] if carry else []
    next_specs, next_shapes = [], []
    if start:
        shapes = [(start, state, inner), (start, 8, inner), (start, 8, wide)]
        next_specs = [anywhere, whole(shapes[1]), whole(shapes[2])]
        next_shapes = [jax.ShapeDtypeStruct(shape, f32) for shape in shapes]
    grid_spec = pltpu.PrefetchScalarGridSpec(
        num_scalar_prefetch=1,
        grid=(count,),
        in_specs=[
            later(inner),
            later(inner),
            later(inner),
            pl.BlockSpec((length, inner), lambda b, *_: (start + top - b, 1)),
            pl.BlockSpec((1, state, inner), lambda b, *_: (start + top - b, 0, 0)),
            later(wide),
            later(wide),
            later(wide),
            later(heads),
            whole(conv_x.shape),
            whole(conv_bc.shape),
            whole((1, heads)),
            whole((1, heads)),
            whole((1, inner)),
            whole(sel.shape),
            whole(sel_t.shape),
        ]
        + carry_specs,
        out_specs=[
            rows(inner),
            rows(wide),
            rows(small - wide),
            whole(conv_x.shape),
            whole(conv_bc.shape),
            whole((1, inner)),
            whole((2, heads)),
        ]
        + next_specs,
        scratch_shapes=[
            pltpu.VMEM((blocks + 1, state, inner), f32),
            pltpu.VMEM((blocks + 1, 8, inner), f32),
            pltpu.VMEM((blocks + 1, 8, wide), f32),
            pltpu.VMEM((3 * length, 2 * heads), bf16),
            pltpu.VMEM((length, length), f32),
            pltpu.VMEM((length, length), f32),
            pltpu.VMEM((length, length), f32),
            pltpu.VMEM((length, length), f32),
            pltpu.VMEM((length, state), f32),
            pltpu.VMEM((length, state), f32),
            pltpu.VMEM((3 * length + 16, sel_t.shape[1]), f32),
            pltpu.VMEM((length, length), f32),
            pltpu.VMEM((length, lanes), f32),
        ],
    )
    return pl.pallas_call(
        functools.partial(backward_kernel, sizes),
        grid_spec=grid_spec,
        out_shape=[
            jax.ShapeDtypeStruct((tokens, inner), bf16),
            jax.ShapeDtypeStruct((tokens, wide), bf16),
            jax.ShapeDtypeStruct((tokens, small - wide), bf16),
            jax.ShapeDtypeStruct(conv_x.shape, f32),
            jax.ShapeDtypeStruct(conv_bc.shape, f32),
            jax.ShapeDtypeStruct((1, inner), f32),
            jax.ShapeDtypeStruct((2, heads), f32),
        ]
        + next_shapes,
        compiler_params=pltpu.CompilerParams(vmem_limit_bytes=VMEM_LIMIT),
        cost_estimate=LIGHT,
        name="ssd_backward",
    )(
        parent, dy, xc, pre, zx, hs, bcc, bcp, bc_pre, dt_raw, conv_x, conv_bc,
        dt_bias[None], a_log[None], skip_l, sel, sel_t, *carry,
    )


def add_kernel(terms, *refs):
    out_refs = refs[terms:]
    size = out_refs[0].shape[0]
    for i, out in enumerate(out_refs):
        rows = slice(i * size, (i + 1) * size)
        total = refs[0][rows, :].astype(f32)
        for ref in refs[1:terms]:
            total = total + ref[rows, :].astype(f32)
        out[...] = total.astype(out.dtype)


def run_add(values, pieces, kind):
    rows, width = values[0].shape
    tile = width // 2 if rows * width > 65536 and width % 256 == 0 else width
    spec = lambda size: pl.BlockSpec((size, tile), lambda j: (0, j))
    size = rows // pieces
    return pl.pallas_call(
        functools.partial(add_kernel, len(values)),
        grid=(width // tile,),
        in_specs=[spec(rows)] * len(values),
        out_specs=[spec(size)] * pieces,
        out_shape=[jax.ShapeDtypeStruct((size, width), kind)] * pieces,
        compiler_params=pltpu.CompilerParams(vmem_limit_bytes=VMEM_LIMIT),
        cost_estimate=LIGHT,
        name="add_parts",
    )(*values)


def mixed_kernel(full, terms, sq_ref, x_ref, *refs):
    length = x_ref.shape[0]
    inv = lax.rsqrt(token_column(sq_ref, pl.program_id(0), length)[:, :1] / full + epsilon)
    total = refs[0][...].astype(f32)
    for ref in refs[1:terms]:
        total = total + ref[...].astype(f32)
    refs[terms][...] = (x_ref[...].astype(f32) + inv * total).astype(bf16)


def run_mixed(squares, x_in, values, full):
    tokens, features = x_in.shape
    blocks, length = squares.shape
    rows = pl.BlockSpec((length, features), lambda b: (b, 0))
    return pl.pallas_call(
        functools.partial(mixed_kernel, full, len(values)),
        grid=(blocks,),
        in_specs=[pl.BlockSpec((blocks, length), lambda b: (0, 0)), rows] + [rows] * len(values),
        out_specs=rows,
        out_shape=jax.ShapeDtypeStruct((tokens, features), bf16),
        compiler_params=pltpu.CompilerParams(vmem_limit_bytes=VMEM_LIMIT),
        cost_estimate=LIGHT,
        name="layer_output",
    )(squares, x_in, *values)


def finish_kernel(terms, x_ref, cot_ref, inv_ref, gain_ref, *refs):
    x = x_ref[...].astype(f32)
    inv = inv_ref[...]
    total = refs[0][...].astype(f32)
    for ref in refs[1:terms]:
        total = total + ref[...].astype(f32)
    gained = total * gain_ref[...]
    spread = inv * inv * inv * jnp.sum(gained * x, axis=1, keepdims=True) / x.shape[1]
    refs[-1][...] = (cot_ref[...].astype(f32) + inv * gained - x * spread).astype(bf16)


def run_finish(values, x_in, cotangent, inv_rms, norm_gain, length):
    tokens, features = x_in.shape
    rows = lambda width: pl.BlockSpec((length, width), lambda b: (b, 0))
    return pl.pallas_call(
        functools.partial(finish_kernel, len(values)),
        grid=(tokens // length,),
        in_specs=[rows(features), rows(features), rows(1), pl.BlockSpec((1, features), lambda b: (0, 0))]
        + [rows(features)] * len(values),
        out_specs=rows(features),
        out_shape=jax.ShapeDtypeStruct((tokens, features), bf16),
        compiler_params=pltpu.CompilerParams(vmem_limit_bytes=VMEM_LIMIT),
        cost_estimate=LIGHT,
        name="input_grad_finish",
    )(x_in, cotangent, inv_rms, norm_gain[None], *values)


def over_columns(left, right):
    return lax.dot_general(left, right, (((1,), (1,)), ((), ())), preferred_element_type=f32)


def after(value, *others):
    return lax.optimization_barrier((value,) + others)[0]


def from_side(value):
    return lax.ppermute(value, "tensor", [(0, 1), (1, 0)])


def side_start(value):
    if lax.axis_size("tensor") == 2:
        return value, from_side(value)
    return None, lax.psum(value, "tensor")


def present(pair):
    return [value for value in pair if value is not None]


def side_total(pair):
    value, got = pair
    return got.astype(f32) if value is None else value.astype(f32) + got.astype(f32)


def pair_up(value, bit):
    size = lax.axis_size("dp")
    return lax.ppermute(value, "dp", [(i, i ^ bit) for i in range(size)])


def dealt_order(bits):
    order = [0]
    for bit in reversed(bits):
        order = order + [j | bit for j in order]
    return order


class Order:
    def __init__(self):
        self.pending = []

    def first(self, value):
        return after(value, *self.pending) if self.pending else value

    def then(self, value):
        self.pending = [value]
        return value

    def wait(self, value):
        self.pending = self.pending + [value]


def send_pieces(pieces, bit):
    return pieces[0], pair_up(pieces[1], bit)


def add_all(order, sent, kind=bf16):
    kept, got = sent
    return order.then(run_add([order.first(kept), got], 1, kind)[0])


def add_send(order, sent, bit):
    kept, got = sent
    pieces = run_add([order.first(kept), got], 2, bf16)
    order.then(pieces[0])
    return send_pieces(pieces, bit)


def add_last(order, sent, bits):
    for bit in bits:
        sent = add_send(order, sent, bit)
    return add_all(order, sent)


def send_same(value, bit):
    return value, pair_up(value, bit)


def local(
    x_in,
    norm_gain,
    w_zx,
    w_bc,
    w_dt,
    conv_x,
    conv_bc,
    dt_bias,
    a_log,
    d_skip,
    gate_gain,
    w_out,
    cotangent,
    block_parent,
):
    tokens, features = x_in.shape
    heads = w_dt.shape[1]
    inner = w_zx.shape[2]
    head_dim = inner // heads
    sides = lax.axis_size("tensor")
    dp = lax.axis_size("dp")
    full = inner * sides
    blocks = block_parent.shape[0]
    length = tokens // blocks
    wide = w_bc.shape[1]
    small = -(-(wide + heads) // 128) * 128
    window = conv_x.shape[0] - 1
    share = features // dp
    me = lax.axis_index("dp")

    near = []
    bit = 2
    while bit < dp:
        near.append(bit)
        bit *= 2
    far = near[1:] + near[:1]

    def places(bits):
        return lax.bitwise_xor(me, jnp.asarray(dealt_order(bits), jnp.int32)).astype(jnp.int32)

    place_near, place_far = places(near), places(far)

    head_of = jnp.arange(inner, dtype=jnp.int32) // head_dim
    one_hot = (jnp.arange(heads, dtype=jnp.int32)[:, None] == head_of[None, :]).astype(bf16)
    sel = jnp.concatenate([one_hot, one_hot], axis=0)
    sel_t = (jnp.arange(128, dtype=jnp.int32)[None, :] == head_of[:, None]).astype(bf16)
    skip_l = jnp.repeat(d_skip, head_dim)[None]

    count = blocks // 2
    step = count * length
    w_dt_t = w_dt.T
    join = lambda values: jnp.concatenate(values, axis=0)

    order = Order()
    normed, turned, inv_rms, bc_pre, dt_raw = run_norm(x_in, cotangent, norm_gain, w_bc, w_dt_t, length)
    turned_near = pair_up(turned, 1)
    w_cat = w_zx.reshape(features, 2 * inner)
    zx = jnp.dot(normed, w_cat, preferred_element_type=f32).astype(bf16)
    dgn = over_columns(after(cotangent, zx), w_out).astype(bf16)
    y, xc, pre, gg, bcc, bcp, hs, sq = run_forward(
        block_parent, bc_pre, dt_raw, zx, dgn, conv_x, conv_bc, dt_bias, a_log, skip_l, gate_gain, sel
    )
    sums = side_start(join([sq[:, 0, :], sq[:, 8, :]]))
    out = jnp.dot(gg, w_out, preferred_element_type=f32).astype(bf16)
    sums = side_total((None if sums[0] is None else after(sums[0], out), sums[1]))
    gg_near = pair_up(gg, 1)
    got_out = side_start(after(out, sums))
    squares, crosses = sums[:blocks], sums[blocks:]
    inv_gate = lax.rsqrt(squares / full + epsilon)
    scale = inv_gate.reshape(1, tokens)
    scale = jnp.concatenate([scale, pair_up(scale, 1)], axis=1)
    dz, dy, gg_grad = run_ungate(squares, crosses, y, zx, dgn, gate_gain, full)
    order.then(dz)
    dz_near = pair_up(dz, 1)
    rights = [order.first(gg), gg_near]
    pieces = run_grad(place_near, 1, turned, turned_near, rights, share, 0, inner, 2, scale)
    order.then(pieces[0])
    w_out_1 = send_pieces(pieces, near[0])
    rights = [order.first(dz), dz_near]
    pieces = run_grad(place_near, 0, turned, turned_near, rights, share, 0, inner, 2)
    order.then(pieces[0])
    w_z_1 = send_pieces(pieces, near[0])

    tail = (conv_x, conv_bc, dt_bias, a_log, skip_l, sel, sel_t, small)
    back = run_backward(
        0, blocks, block_parent, order.first(dy), xc, pre, zx, hs, bcc, bcp, bc_pre, dt_raw, *tail, ()
    )
    dx, dbc, ddt, gkx, gkbc, gskip, ghead = back
    order.then(dx)
    order.wait(got_out[1])
    order.wait(w_out_1[1])
    w_out_2 = add_send(order, w_out_1, near[1])
    dx_near = pair_up(dx, 1)
    got_bc = side_start(dbc)
    low, low_gain = run_input(dz, order.first(dx), dbc, ddt, w_cat, w_bc, w_dt_t, x_in, inv_rms, 0, tokens)
    order.then(low)
    got_low = side_start(low)
    w_out_3 = add_send(order, w_out_2, near[2])
    got_bc = tuple(None if value is None else order.first(value) for value in got_bc)
    d_small = jnp.concatenate([side_total(got_bc).astype(bf16), ddt], axis=1)
    order.then(d_small)
    small_near = pair_up(d_small, 1)
    edge = inner * 5 // 8 // 256 * 256
    pieces = run_grad(place_near, 0, turned, turned_near, [order.first(dx), dx_near], share, 0, edge, 2)
    order.then(pieces[1])
    w_z_2 = add_send(order, w_z_1, near[1])
    sent_a = send_pieces(pieces, near[0])
    pieces = run_grad(place_near, 0, turned, turned_near, [order.first(d_small), small_near], share, 0, small, 2)
    order.then(pieces[1])
    sent_s = send_pieces(pieces, near[0])
    pieces = run_grad(place_far, 0, turned, turned_near, [order.first(dx), dx_near], share, edge, inner - edge, 2)
    order.then(pieces[1])
    w_out_grad = add_last(order, w_out_3, near[3:])
    sent_b = send_pieces(pieces, far[0])

    def spread_rows(sent, bit):
        kept, got = sent
        places_s.extend([j ^ bit for j in places_s])
        return order.then(join([order.first(kept), got]))

    places_s = [0]
    sent_a = add_send(order, sent_a, near[1])
    sent_s = add_send(order, sent_s, near[1])
    w_z_3 = add_send(order, w_z_2, near[2])
    mixed = order.then(run_mixed(squares, order.first(x_in), present(got_out), full))
    low_gain, gkbc, gskip, gkx, ghead, gg_grad = order.first((low_gain, gkbc, gskip, gkx, ghead, gg_grad))
    shared = jnp.concatenate([low_gain.reshape(-1), gkbc.reshape(-1)])
    d_skip_part = jnp.sum(gskip.reshape(heads, head_dim), axis=1)
    own = jnp.concatenate(
        [gkx.reshape(-1), ghead.reshape(-1), d_skip_part, gg_grad.reshape(-1)]
    )
    n_shared, n_own = shared.shape[0], own.shape[0]
    pad_shared = -(-n_shared // 1024) * 1024
    pad_own = -(-n_own // 1024) * 1024
    shared = jnp.concatenate([shared, jnp.zeros((pad_shared - n_shared,), f32)]).reshape(-1, 128)
    own = jnp.concatenate([own, jnp.zeros((pad_own - n_own,), f32)]).reshape(-1, 128)
    packed = join([shared, own])

    order.then(packed)
    packed = send_same(packed, 1)
    sent_b = add_send(order, sent_b, far[1])
    packed = send_same(add_all(order, packed, f32), near[0])
    sent_a = add_send(order, sent_a, near[2])
    sent_s = add_send(order, sent_s, near[2])
    packed = send_same(add_all(order, packed, f32), near[1])
    w_z_grad = add_last(order, w_z_3, near[3:])
    w_s = add_last(order, sent_s, near[3:])
    rows_bc = send_same(w_s[:, :wide], near[2])
    sent_b = add_send(order, sent_b, far[2])
    packed = send_same(add_all(order, packed, f32), near[2])
    rows_bc = send_same(spread_rows(rows_bc, near[2]), near[1])
    w_x_a = add_last(order, sent_a, near[3:])
    packed = add_all(order, packed, f32)
    for bit in near[3:]:
        packed = add_all(order, send_same(packed, bit), f32)
    got_shared = side_start(packed[: pad_shared // 128])
    rows_bc = send_same(spread_rows(rows_bc, near[1]), near[0])
    values = present(got_low)
    input_grad = order.then(
        run_finish([order.first(values[0])] + values[1:], x_in, cotangent, inv_rms, norm_gain, length)
    )
    w_x_b = add_last(order, sent_b, far[3:])
    rows_bc = spread_rows(rows_bc, near[0])
    for bit in near[3:]:
        rows_bc = spread_rows(send_same(rows_bc, bit), bit)
    rows_bc = spread_rows(send_same(rows_bc, 1), 1)
    chunks = rows_bc.reshape(dp, share, wide)
    back_to = jnp.asarray([places_s.index(j) for j in range(dp)], jnp.int32)
    w_bc_grad = jnp.take(chunks, back_to[lax.bitwise_xor(me, jnp.arange(dp, dtype=jnp.int32))], axis=0)
    w_bc_grad = w_bc_grad.reshape(features, wide).astype(f32)
    w_dt_grad = w_s[:, wide : wide + heads].astype(f32)
    w_x_grad = jnp.concatenate([w_x_a, w_x_b], axis=1)
    shared = side_total(got_shared).reshape(-1)
    own = packed[pad_shared // 128 :].reshape(-1)

    edge = (window + 1) * inner
    w_zx_grad = jnp.stack([w_z_grad, w_x_grad], axis=1).astype(f32)
    return (
        mixed,
        input_grad,
        shared[:features],
        w_zx_grad,
        w_bc_grad,
        w_dt_grad,
        own[:edge].reshape(window + 1, inner),
        shared[features:n_shared].reshape(window + 1, wide),
        own[edge : edge + heads],
        own[edge + heads : edge + 2 * heads],
        own[edge + 2 * heads : edge + 3 * heads],
        own[edge + 3 * heads : n_own],
        w_out_grad.astype(f32).T,
    )


def solution(mesh):
    return jax.shard_map(
        local,
        mesh=mesh,
        in_specs=(
            P("dp", None),
            P(),
            P(None, None, "tensor"),
            P(),
            P(None, "tensor"),
            P(None, "tensor"),
            P(),
            P("tensor"),
            P("tensor"),
            P("tensor"),
            P("tensor"),
            P("tensor", None),
            P("dp", None),
            P("dp"),
        ),
        out_specs=(
            P("dp", None),
            P("dp", None),
            P(),
            P("dp", None, "tensor"),
            P(),
            P("dp", "tensor"),
            P(None, "tensor"),
            P(),
            P("tensor"),
            P("tensor"),
            P("tensor"),
            P("tensor"),
            P("tensor", "dp"),
        ),
        check_vma=False,
    )
```
